128 devices in a mesh: src: 32 (over y, z, core), rcv: 4 (over x).
Axes of the slice: x: 4, y: 4, z: 4, core: 2. Of those that a mesh axis runs over, the one named last changes fastest.
Arguments:
- traces: bfloat16 [262144, 2048], P(('src', 'rcv'))
- trace_source: int32 [262144], P(('src', 'rcv')), may hold values from 0 to 255, as said below
- trace_offset: int32 [262144], P(('src', 'rcv')), may hold values from 0 to 63
- trace_slot: int32 [262144], P(('src', 'rcv')), may hold values from 0 to 1023, as said below
- request_list: int32 [128, 128, 8], P(('src', 'rcv')), may hold values from 0 to 63, as said below
- source_terms: float32 [256, 1024], P('src'), may hold values from -3 to 3
- receiver_terms: float32 [8192, 1024], P(('src', 'rcv')), may hold values from -3 to 3
- offset_terms: float32 [64, 1024], replicated, may hold values from -3 to 3
Outputs:
- source_new: float32 [256, 1024], P('src')
- receiver_new: float32 [8192, 1024], P(('src', 'rcv'))
- offset_new: float32 [64, 1024], replicated
The draws below stay inside these ranges and needn't reach their ends.
Inputs may be any that keep to these rules, and one draw needn't show every extreme that they name: `trace_source`: trace t's source is one of the 8 sources of the src index that holds t. `request_list`: within one device's list for one owner the 8 entries are distinct. `trace_slot`: a slot names an owner and a position in the holding device's own request list.
All inputs are finite; a program needn't handle non-finite values.
Results may differ from the reference program's by a relative error of at most 0.0023.
Values sent between devices are 32-bit elements; how exact they have to be, the bound alone decides.
A program may use at most 128 MiB of HBM per device.

```python
import math
import jax
import jax.numpy as jnp
from jax import lax

NS = 2048
F = 1024
TR_DEV = 2048
SRC_DEV = 8
RCV_DEV = 64
CAP = 8
NOFF = 64
PEERS = 128
TRACES = 262144
NSRC = 256
NRCV = 8192


def request_plan(key):
    base = jax.random.fold_in(key, 7)
    key_count, key_full, key_order, key_owner, key_pick = jax.random.split(base, 5)
    counts = jax.random.randint(key_count, (PEERS, PEERS), 1, CAP + 1)
    full = jax.random.randint(key_full, (PEERS,), 0, PEERS)
    full = full.at[0].set(PEERS - 1)
    column = jnp.arange(PEERS, dtype=jnp.int32)[None, :]
    counts = jnp.where(column == full[:, None], CAP, counts).astype(jnp.int32)
    scores = jax.random.randint(key_order, (PEERS, PEERS, RCV_DEV), 0, 2 ** 20)
    scores = scores * RCV_DEV + jnp.arange(RCV_DEV, dtype=jnp.int32)[None, None, :]
    scores = scores.at[0, 0, RCV_DEV - 1].set(-1)
    lists = jnp.argsort(scores, axis=2)[:, :, :CAP].astype(jnp.int32)
    device = (jnp.arange(TRACES, dtype=jnp.int32) // TR_DEV).astype(jnp.int32)
    owner = jax.random.randint(key_owner, (TRACES,), 0, PEERS).astype(jnp.int32)
    owner = owner.at[0].set(PEERS - 1)
    live = counts[device, owner]
    within = jax.random.randint(key_pick, (TRACES,), 0, live).astype(jnp.int32)
    within = within.at[0].set(CAP - 1)
    slots = (owner * CAP + within).astype(jnp.int32)
    return (lists, slots)


def draw_request_list(key, part):
    return request_plan(key)[0]


def draw_trace_slot(key, part):
    return request_plan(key)[1]


def draw_trace_source(key, part):
    per_group = TRACES * SRC_DEV // NSRC
    group = (jnp.arange(TRACES, dtype=jnp.int32) // per_group).astype(jnp.int32)
    pick = jax.random.randint(jax.random.fold_in(key, 11), (TRACES,), 0, SRC_DEV)
    return (group * SRC_DEV + pick).astype(jnp.int32)


def draw_traces(key, part):
    key_a, key_b = jax.random.split(jax.random.fold_in(key, 13), 2)
    device = (jnp.arange(TRACES) // TR_DEV).astype(jnp.float32)
    rise = 3.0 ** (device / max(PEERS - 1, 1))
    spread = jnp.exp(jax.random.uniform(key_b, (TRACES,), jnp.float32, -0.7, 0.7))
    samples = jnp.clip(jax.random.normal(key_a, (TRACES, NS), jnp.float32), -6.0, 6.0)
    return (samples * (rise * spread)[:, None]).astype(jnp.bfloat16)


def plant(array, rng, low, top_value):
    longest = array.shape.index(max(array.shape))
    spots = []
    for shift in (0, 1):
        where = [jax.random.randint(jax.random.fold_in(rng, axis), (), 0, length) for axis, length in enumerate(array.shape)]
        where[longest] = (where[longest] + shift) % array.shape[longest]
        spots.append(tuple(where))
    return array.at[spots[0]].set(low).at[spots[1]].set(top_value)


def shard_levels(stream_key, extent, pieces, smallest, top_value):
    loudness, own = 1.0, jax.random.fold_in(stream_key, 6)
    for axis_at, shards_of in pieces:
        heights = jnp.exp(jax.random.uniform(jax.random.fold_in(own, axis_at), (shards_of,), jnp.float32, smallest / len(pieces), top_value / len(pieces)))
        loudness = loudness * jnp.repeat(heights, extent[axis_at] // shards_of).reshape([-1 if axis == axis_at else 1 for axis in range(len(extent))])
    return loudness


def noise(stream_key, extent, deviation, most, cuts=(), held_as=jnp.bfloat16):
    loudness = shard_levels(stream_key, extent, cuts, -0.22, 0.18) if cuts else 1.0
    result = jax.random.normal(stream_key, extent, jnp.float32) * deviation * loudness
    return jnp.minimum(jnp.maximum(result, -most), most).astype(held_as)


def setup_inputs(seed: int = 0) -> dict:
    key_of = jax.random.split(jax.random.key(seed), 9)
    return {
        "traces": draw_traces(jax.random.fold_in(key_of[8], 71), 0),
        "trace_source": draw_trace_source(jax.random.fold_in(key_of[8], 71), 0),
        "trace_offset": plant(jax.random.randint(key_of[2], (TRACES,), 0, NOFF), jax.random.fold_in(key_of[2], 1), 0, NOFF - 1).astype(jnp.int32),
        "trace_slot": draw_trace_slot(jax.random.fold_in(key_of[8], 71), 0),
        "request_list": draw_request_list(jax.random.fold_in(key_of[8], 71), 0),
        "source_terms": noise(key_of[5], (NSRC, F), 0.5, 3.0, ((0, 32),), jnp.float32),
        "receiver_terms": noise(key_of[6], (NRCV, F), 0.5, 3.0, ((0, 128),), jnp.float32),
        "offset_terms": noise(key_of[7], (NOFF, F), 0.5, 3.0, (), jnp.float32),
    }


def dft_table(samples):
    freq = samples // 2
    index_n = lax.broadcasted_iota(jnp.int32, (samples, freq), 0)
    index_f = lax.broadcasted_iota(jnp.int32, (samples, freq), 1)
    phase = (index_n * index_f % samples).astype(jnp.float32) * (2.0 * math.pi / samples)
    taper = 0.5 - 0.5 * jnp.cos((index_n.astype(jnp.float32) + 0.5) * (2.0 * math.pi / samples))
    scaled = taper / math.sqrt(samples)
    return jnp.concatenate([scaled * jnp.cos(phase), -scaled * jnp.sin(phase)], axis=1).astype(jnp.bfloat16)

def log_amp(block, table):
    freq = table.shape[1] // 2
    spectra = jnp.dot(block, table, preferred_element_type=jnp.float32)
    real_part = spectra[:, :freq]
    imag_part = spectra[:, freq:]
    return 0.5 * jnp.log(real_part * real_part + imag_part * imag_part + 0.01)

def reference(traces, trace_source, trace_offset, trace_slot, request_list, source_terms, receiver_terms, offset_terms):
    table = dft_table(NS)
    blocks = traces.reshape(PEERS, TR_DEV, NS)
    logamp = lax.map(lambda blk: log_amp(blk, table), blocks).reshape(TRACES, F)
    device = (jnp.arange(TRACES, dtype=jnp.int32) // TR_DEV).astype(jnp.int32)
    owner = (trace_slot // CAP).astype(jnp.int32)
    within = (trace_slot % CAP).astype(jnp.int32)
    receiver = (owner * RCV_DEV + request_list[device, owner, within]).astype(jnp.int32)
    residual = logamp - source_terms[trace_source] - receiver_terms[receiver] - offset_terms[trace_offset]
    ones = jnp.ones((TRACES,), jnp.float32)
    src_sum = jax.ops.segment_sum(residual, trace_source, num_segments=NSRC)
    src_cnt = jax.ops.segment_sum(ones, trace_source, num_segments=NSRC)
    rcv_sum = jax.ops.segment_sum(residual, receiver, num_segments=NRCV)
    rcv_cnt = jax.ops.segment_sum(ones, receiver, num_segments=NRCV)
    off_sum = jax.ops.segment_sum(residual, trace_offset, num_segments=NOFF)
    off_cnt = jax.ops.segment_sum(ones, trace_offset, num_segments=NOFF)
    source_new = source_terms + src_sum / (src_cnt + 1.0)[:, None]
    receiver_new = receiver_terms + rcv_sum / (rcv_cnt + 1.0)[:, None]
    offset_new = offset_terms + off_sum / (off_cnt + 1.0)[:, None]
    return (source_new, receiver_new, offset_new)
```

```python
import functools
import math

import jax
import jax.numpy as jnp
from jax import lax
from jax.experimental import pallas as pl
from jax.experimental.pallas import tpu as pltpu
from jax.sharding import PartitionSpec as P

NS = 2048
LANES = 128
ROWS = 1152
STEP = 2.0 * math.pi / NS
NT = (((1,), (1,)), ((), ()))


def trig_base(cb, sb):
    row = lax.broadcasted_iota(jnp.int32, (128, LANES), 0)
    col = lax.broadcasted_iota(jnp.int32, (128, LANES), 1)
    far = ((row * 16 * col) % NS).astype(jnp.float32) * STEP
    far_c, far_s = jnp.cos(far), jnp.sin(far)
    wide = (row * 16).astype(jnp.float32) * STEP
    wide_c, wide_s = jnp.cos(wide), jnp.sin(wide)
    row = lax.broadcasted_iota(jnp.int32, (16, LANES), 0)
    col = lax.broadcasted_iota(jnp.int32, (16, LANES), 1)
    near = ((row * col) % NS).astype(jnp.float32) * STEP
    near_c, near_s = jnp.cos(near), jnp.sin(near)
    half = (row.astype(jnp.float32) + 0.5) * STEP
    half_c, half_s = jnp.cos(half), jnp.sin(half)
    for b in range(128):
        fc, fs = far_c[b : b + 1], far_s[b : b + 1]
        wc, ws = wide_c[b : b + 1], wide_s[b : b + 1]
        taper = (0.5 - 0.5 * (wc * half_c - ws * half_s)) * (1.0 / math.sqrt(NS))
        cb[16 * b : 16 * b + 16, :] = taper * (fc * near_c - fs * near_s)
        sb[16 * b : 16 * b + 16, :] = taper * (fs * near_c + fc * near_s)


def chunk_table(c, rows, cb, sb, table):
    n = lax.broadcasted_iota(jnp.int32, (16, LANES), 0)
    turn = ((n * c) % 16).astype(jnp.float32) * (2.0 * math.pi / 16.0)
    tc, ts = jnp.cos(turn), jnp.sin(turn)
    for r in rows:
        bc, bs = cb[r : r + 16, :], sb[r : r + 16, :]
        table[r : r + 16, 0:LANES] = (bc * tc - bs * ts).astype(jnp.bfloat16)
        table[r : r + 16, LANES : 2 * LANES] = (-(bs * tc + bc * ts)).astype(jnp.bfloat16)


def split(x):
    upper = x.astype(jnp.bfloat16)
    return upper, (x - upper.astype(jnp.float32)).astype(jnp.bfloat16)


def local_kernel(idx, tr_hbm, src, off, sums, counts, tr, hot, table, cb, sb, low, sem):
    cp = pltpu.make_async_copy(tr_hbm, tr, sem)
    cp.start()
    trig_base(cb, sb)

    slot, first, second = idx[0:1, :], idx[1:2, :], idx[2:3, :]

    def hot_rows(i, _):
        r = pl.multiple_of(i * 32, 32)
        row = lax.broadcasted_iota(jnp.int32, (32, NS), 0) + r
        hit = (row == slot) | (row == first) | (row == second)
        hot[pl.ds(r, 32), 0:NS] = jnp.where(hit, 1.0, 0.0).astype(jnp.bfloat16)
        return 0

    lax.fori_loop(0, ROWS // 32, hot_rows, 0)
    cnt = lax.dot_general(hot[:, 0:NS], hot[1024:ROWS, 0:NS], NT, preferred_element_type=jnp.float32)
    counts[...] = cnt
    upper, lower = split(cnt)
    hot[:, NS : NS + LANES] = upper
    hot[:, NS + LANES : NS + 2 * LANES] = lower
    low[NS + 72 : NS + 128, :] = jnp.zeros((56, 2 * LANES), jnp.bfloat16)
    low[NS + 200 : NS + 256, :] = jnp.zeros((56, 2 * LANES), jnp.bfloat16)
    cp.wait()

    def chunk(c, _):
        lane = pl.multiple_of(c * LANES, LANES)
        chunk_table(c, range(0, NS, 16), cb, sb, table)
        for r in range(0, NS, 256):
            spec = jnp.dot(tr[r : r + 256, :], table[...], preferred_element_type=jnp.float32)
            re, im = spec[:, 0:LANES], spec[:, LANES:]
            amp = 0.5 * jnp.log(re * re + im * im + 0.01)
            upper, lower = split(amp)
            low[r : r + 256, 0:LANES] = upper
            low[r : r + 256, LANES:] = lower
        terms = jnp.concatenate([src[:, pl.ds(lane, LANES)], off[:, pl.ds(lane, LANES)]], axis=0)
        upper, lower = split(-terms)
        for r in (NS, NS + LANES):
            low[r : r + 72, 0:LANES] = upper
            low[r : r + 72, LANES:] = lower
        for r in range(0, ROWS, 384):
            out = jnp.dot(hot[r : r + 384, :], low[...], preferred_element_type=jnp.float32)
            sums[r : r + 384, pl.ds(lane, LANES)] = out[:, 0:LANES] + out[:, LANES:]
        return 0

    lax.fori_loop(0, 8, chunk, 0)


def local_sums(idx, traces, src, off):
    vmem = pl.BlockSpec(memory_space=pltpu.VMEM)
    return pl.pallas_call(
        local_kernel,
        out_shape=(
            jax.ShapeDtypeStruct((ROWS, 1024), jnp.float32),
            jax.ShapeDtypeStruct((ROWS, LANES), jnp.float32),
        ),
        in_specs=[vmem, pl.BlockSpec(memory_space=pl.ANY), vmem, vmem],
        out_specs=(vmem, vmem),
        scratch_shapes=[
            pltpu.VMEM((NS, NS), jnp.bfloat16),
            pltpu.VMEM((ROWS, NS + 256), jnp.bfloat16),
            pltpu.VMEM((NS, 256), jnp.bfloat16),
            pltpu.VMEM((NS, LANES), jnp.float32),
            pltpu.VMEM((NS, LANES), jnp.float32),
            pltpu.VMEM((NS + 256, 256), jnp.bfloat16),
            pltpu.SemaphoreType.DMA,
        ],
        compiler_params=pltpu.CompilerParams(vmem_limit_bytes=56 << 20),
        name="local_sums",
    )(idx, traces, src, off)


def local(traces, trace_source, trace_offset, trace_slot, request_list, src, rcv, off):
    axes = ("src", "rcv")
    s = lax.axis_index("src")
    first = trace_source - s * 8 + 1024
    idx = jnp.stack([trace_slot, first, trace_offset + 1032])
    idx = jnp.concatenate([idx, jnp.zeros((5, NS), jnp.int32)])
    sums, counts = local_sums(idx, traces, src, off)
    hi = lax.Precision.HIGHEST
    asked = lax.all_to_all(request_list.reshape(128, 8), axes, split_axis=0, concat_axis=0, tiled=True)
    got_cnt = lax.all_to_all(
        counts[:1024].reshape(128, 8, LANES), axes, split_axis=0, concat_axis=0, tiled=True
    ).reshape(1024, LANES)
    got = lax.all_to_all(
        sums[:1024].reshape(128, 8, 1024), axes, split_axis=0, concat_axis=0, tiled=True
    ).reshape(1024, 1024)
    dense = (asked.reshape(1, 1024) == jnp.arange(64)[:, None]).astype(jnp.float32)
    wide = jnp.tile(got_cnt[:, 0:8], (1, 32)) * (
        (jnp.arange(1024) // 32)[:, None] == (jnp.arange(256) // 8)[None, :]
    )
    n_src = jnp.dot(dense, wide, precision=hi)
    n_off = jnp.dot(dense, got_cnt[:, 8:72], precision=hi)
    tot = jnp.sum(n_off, axis=1)
    rsum = jnp.dot(dense, got, precision=hi)
    receiver_new = (rcv + rsum) / (tot + 1.0)[:, None]
    u_src = jnp.dot(n_src.T, rcv, precision=hi)
    u_off = jnp.dot(n_off.T, rcv, precision=hi)
    u_part = lax.psum_scatter(u_src, "src", scatter_dimension=0, tiled=True)
    src_sum, src_cnt = lax.psum((sums[1024:1032] - u_part, jnp.sum(counts[1024:1032, 8:72], axis=1)), "rcv")
    off_sum, off_cnt = lax.psum((sums[1032:1096] - u_off, jnp.sum(counts[1032:1096, 0:8], axis=1)), axes)
    source_new = src + src_sum / (src_cnt + 1.0)[:, None]
    offset_new = off + off_sum / (off_cnt + 1.0)[:, None]
    return (source_new, receiver_new, offset_new)


def solution(mesh):
    every = P(("src", "rcv"))
    return jax.shard_map(
        local,
        mesh=mesh,
        in_specs=(P(("src", "rcv"), None), every, every, every, P(("src", "rcv"), None, None), P("src", None), P(("src", "rcv"), None), P()),
        out_specs=(P("src", None), P(("src", "rcv"), None), P()),
        check_vma=False,
    )
```

```python
import math

import jax
import jax.numpy as jnp
from jax import lax
from jax.experimental import pallas as pl
from jax.experimental.pallas import tpu as pltpu
from jax.sharding import PartitionSpec as P

NS = 2048
LANES = 128
ROWS = 1152
WIDE = 1024 + LANES
MESH = pl.DeviceIdType.MESH
KINDS = (0, 1, 2, 0, 1, 2, 0, 1)
SECOND = ("y", "z", "x")
THIRD = ("z", "x", "y")
TN = (((0,), (0,)), ((), ()))
STEP = 2.0 * math.pi / NS
NT = (((1,), (1,)), ((), ()))


def trig_base(cb, sb):
    row = lax.broadcasted_iota(jnp.int32, (128, LANES), 0)
    col = lax.broadcasted_iota(jnp.int32, (128, LANES), 1)
    far = ((row * 16 * col) % NS).astype(jnp.float32) * STEP
    far_c, far_s = jnp.cos(far), jnp.sin(far)
    wide = (row * 16).astype(jnp.float32) * STEP
    wide_c, wide_s = jnp.cos(wide), jnp.sin(wide)
    row = lax.broadcasted_iota(jnp.int32, (16, LANES), 0)
    col = lax.broadcasted_iota(jnp.int32, (16, LANES), 1)
    near = ((row * col) % NS).astype(jnp.float32) * STEP
    near_c, near_s = jnp.cos(near), jnp.sin(near)
    half = (row.astype(jnp.float32) + 0.5) * STEP
    half_c, half_s = jnp.cos(half), jnp.sin(half)
    for b in range(128):
        fc, fs = far_c[b : b + 1], far_s[b : b + 1]
        wc, ws = wide_c[b : b + 1], wide_s[b : b + 1]
        taper = (0.5 - 0.5 * (wc * half_c - ws * half_s)) * (1.0 / math.sqrt(NS))
        cb[16 * b : 16 * b + 16, :] = taper * (fc * near_c - fs * near_s)
        sb[16 * b : 16 * b + 16, :] = taper * (fs * near_c + fc * near_s)


def chunk_table(c, rows, cb, sb, table):
    n = lax.broadcasted_iota(jnp.int32, (16, LANES), 0)
    turn = ((n * c) % 16).astype(jnp.float32) * (2.0 * math.pi / 16.0)
    tc, ts = jnp.cos(turn), jnp.sin(turn)
    for r in rows:
        bc, bs = cb[r : r + 16, :], sb[r : r + 16, :]
        table[r : r + 16, 0:LANES] = (bc * tc - bs * ts).astype(jnp.bfloat16)
        table[r : r + 16, LANES : 2 * LANES] = (-(bs * tc + bc * ts)).astype(jnp.bfloat16)


def split(x):
    upper = x.astype(jnp.bfloat16)
    return upper, (x - upper.astype(jnp.float32)).astype(jnp.bfloat16)


def kernel(
    tr_hbm, slot_ref, src_ref, off_ref, list_ref, s_ref, r_ref, o_ref,
    snew, rnew, onew,
    tr, hot, table, cb, sb, low, extra,
    grid, b1, b1d, b2, b2d, b3, pick,
    c2, c3, us, e0, e1, v2, e2, uoff,
    ex, off, eo, ho, eh, eh2, eh3, fa, inv,
    tr_sem, s0s, s0r, s1s, s1r, s2s, s2r, s3s, s3r, us_s, us_r, os_s, os_r, xs_s, xs_r,
):
    f32, bf16 = jnp.float32, jnp.bfloat16
    group, x = lax.axis_index("src"), lax.axis_index("rcv")
    c, z, y = lax.rem(group, 2), lax.rem(group // 2, 4), group // 8
    me = {"x": x, "y": y, "z": z}

    def at(ax, k, flip=False):
        p = dict(me)
        if ax:
            p[ax] = lax.rem(p[ax] + k, 4)
        core = 1 - c if flip else c
        return ((p["y"] * 4 + p["z"]) * 2 + core, p["x"])

    def step(ax, k):
        return lax.rem(me[ax] + k, 4)

    twin = at(None, 0, True)
    peers = [twin] + [at(ax, k) for ax in "xyz" for k in (1, 2, 3)] + [at("x", k, True) for k in (1, 2, 3)]
    barrier = pltpu.get_barrier_semaphore()
    for p in peers:
        pl.semaphore_signal(barrier, inc=1, device_id=p, device_id_type=MESH)

    load = pltpu.make_async_copy(tr_hbm, tr, tr_sem)
    load.start()

    def rc(a, b, ss, rs, dev):
        return pltpu.make_async_remote_copy(
            src_ref=a, dst_ref=b, send_sem=ss, recv_sem=rs, device_id=dev, device_id_type=MESH
        )

    def start(copies):
        for cp in copies:
            cp.start()

    def wait(copies):
        for cp in copies:
            cp.wait()

    def x0(i):
        return [rc(grid.at[i, 2], grid.at[i, 1], s0s.at[i], s0r.at[i], twin)]

    def x1(i, kind, n):
        out = []
        for k in (1, 2, 3):
            j = step("xyz"[kind], k)
            part = (grid.at[i, 0:2, :, :, j], grid.at[i, 0:2, j], grid.at[i, 0:2, :, j])[kind]
            out.append(rc(part, b1.at[n, k - 1], s1s.at[n, k - 1], s1r.at[n, k - 1], at("xyz"[kind], k)))
        return out

    def x2(i, kind):
        ax = SECOND[kind]
        return [
            rc(b1d.at[i, step(ax, k)], b2.at[i, k - 1], s2s.at[i, k - 1], s2r.at[i, k - 1], at(ax, k))
            for k in (1, 2, 3)
        ]

    def x3(i, kind):
        ax = THIRD[kind]
        return [
            rc(b2d.at[i, step(ax, k)], b3.at[i, k - 1], s3s.at[i, k - 1], s3r.at[i, k - 1], at(ax, k))
            for k in (1, 2, 3)
        ]

    def c_x2():
        return [
            rc(b1d.at[8, step("y", k)], c2.at[k], s2s.at[8, k - 1], s2r.at[8, k - 1], at("y", k)) for k in (1, 2, 3)
        ]

    def c_x3():
        return [
            rc(c2.at[:, step("z", k)], c3.at[k - 1], s3s.at[8, k - 1], s3r.at[8, k - 1], at("z", k)) for k in (1, 2, 3)
        ]

    def u_core():
        return [rc(us.at[1], e0, us_s.at[0], us_r.at[0], twin)]

    def u_y():
        return [rc(us.at[0, :, k], e1.at[k - 1], us_s.at[k], us_r.at[k], at("y", 4 - k)) for k in (1, 2, 3)]

    def u_z():
        return [rc(v2.at[k], e2.at[k - 1], us_s.at[3 + k], us_r.at[3 + k], at("z", 4 - k)) for k in (1, 2, 3)]

    def src_x():
        return [rc(ex.at[x], ex.at[x], xs_s.at[k - 1], xs_r.at[k - 1], at("x", k)) for k in (1, 2, 3)]

    def off_core():
        return [rc(off.at[1 - c], eo, os_s.at[0], os_r.at[0], twin)]

    def off_x():
        return [rc(ho.at[step("x", k)], eh.at[k - 1], os_s.at[k], os_r.at[k], at("x", k)) for k in (1, 2, 3)]

    def off_y():
        return [rc(eh2.at[y], eh2.at[y], os_s.at[3 + k], os_r.at[3 + k], at("y", k)) for k in (1, 2, 3)]

    def off_z():
        return [rc(eh3.at[z], eh3.at[z], os_s.at[6 + k], os_r.at[6 + k], at("z", k)) for k in (1, 2, 3)]

    def off_all():
        to = [at("x", k) for k in (1, 2, 3)] + [twin] + [at("x", k, True) for k in (1, 2, 3)]
        return [rc(fa.at[c, x], fa.at[c, x], os_s.at[10 + n], os_r.at[10 + n], d) for n, d in enumerate(to)]

    s = slot_ref[...]
    row_of = (
        (((s >> 5) & 1) ^ c) * 512 + (s >> 8) * 128 + ((s >> 6) & 3) * 32 + ((s >> 3) & 3) * 8 + (s & 7)
    )
    first = src_ref[...] - group * 8 + 1024
    second = off_ref[...] + 1032

    def hot_rows(i, _):
        r = pl.multiple_of(i * 32, 32)
        row = lax.broadcasted_iota(jnp.int32, (32, LANES), 0) + r
        for b in range(16):
            hit = row == row_of[b : b + 1, :]
            hot[pl.ds(r, 32), b * LANES : (b + 1) * LANES] = jnp.where(hit, 1.0, 0.0).astype(bf16)
        return 0

    lax.fori_loop(0, 32, hot_rows, 0)
    for r in range(1024, ROWS, 32):
        row = lax.broadcasted_iota(jnp.int32, (32, LANES), 0) + r
        for b in range(16):
            hit = (row == first[b : b + 1, :]) | (row == second[b : b + 1, :])
            hot[r : r + 32, b * LANES : (b + 1) * LANES] = jnp.where(hit, 1.0, 0.0).astype(bf16)

    cnt = lax.dot_general(hot[:, 0:NS], hot[1024:ROWS, 0:NS], NT, preferred_element_type=f32)
    upper, lower = split(cnt)
    hot[:, NS : NS + LANES] = upper
    hot[:, NS + LANES : NS + 2 * LANES] = lower
    low[NS + 72 : NS + 128, :] = jnp.zeros((56, 2 * LANES), bf16)
    low[NS + 200 : NS + 256, :] = jnp.zeros((56, 2 * LANES), bf16)
    lane = lax.broadcasted_iota(jnp.int32, (1, LANES), 1)
    count_s = jnp.sum(jnp.where((lane >= 8) & (lane < 72), cnt[1024:1032], 0.0), axis=1, keepdims=True)
    count_o = jnp.sum(jnp.where(lane < 8, cnt[1032:1096], 0.0), axis=1, keepdims=True)
    extra[0:8, 1024:WIDE] = jnp.broadcast_to(count_s, (8, LANES))
    extra[8:72, 1024:WIDE] = jnp.broadcast_to(count_o, (64, LANES))

    asked = list_ref[...].astype(f32)
    for yy in range(4):
        for zz in range(4):
            for xx in range(4):
                p = (yy * 4 + zz) * 8 + xx
                even = jnp.broadcast_to(asked[:, p : p + 1], (8, LANES))
                odd = jnp.broadcast_to(asked[:, p + 4 : p + 5], (8, LANES))
                own, far = jnp.where(c == 0, even, odd), jnp.where(c == 0, odd, even)
                r = ((yy * 4 + zz) * 4 + xx) * 8
                grid[8, 0, yy, zz, xx] = jnp.where(lane == 80 + 8, own, cnt[r : r + 8])
                q = cnt[512 + r : 520 + r]
                moved = jnp.where((lane >= 80) & (lane < 88), pltpu.roll(q, 80, 1), jnp.where(lane < 8, 0.0, q))
                grid[8, 2, yy, zz, xx] = jnp.where(lane == 80 + 8, far, moved)

    pl.semaphore_wait(barrier, len(peers))
    start(x0(8))
    trig_base(cb, sb)
    load.wait()

    def rows64(i, n, kind, p, q):
        own = (
            grid[i, 0:2, p, q, x] if kind == 0 else grid[i, 0:2, y, p, q] if kind == 1 else grid[i, 0:2, p, z, q]
        )
        return jnp.concatenate([own.reshape(16, LANES), b1[n, :, :, p, q].reshape(48, LANES)], axis=0)

    def densify(i, n, kind):
        def one(m, _):
            p, q = m // 4, lax.rem(m, 4)
            upper, lower = split(rows64(i, n, kind, p, q))
            both = jnp.concatenate([upper, lower], axis=1)
            out = jnp.dot(pick[kind, m], both, preferred_element_type=f32)
            total = out[:, 0:LANES] + out[:, LANES:]
            if kind == 2:
                b1d[i, q, p] = total
            else:
                b1d[i, p, q] = total
            return 0

        lax.fori_loop(0, 16, one, 0, unroll=4)

    def counts_1():
        wait(x0(8))
        for kind in range(3):
            start(x1(8, kind, 8 + kind))

    def counts_2():
        eye = jnp.where(
            lax.broadcasted_iota(jnp.int32, (64, 64), 0) == lax.broadcasted_iota(jnp.int32, (64, 64), 1), 1.0, 0.0
        ).astype(bf16)
        col = lax.broadcasted_iota(jnp.int32, (64, 64), 1).astype(f32)
        for kind in range(3):
            wait(x1(8, kind, 8 + kind))

            def one(m, _, kind=kind):
                rows = rows64(8, 8 + kind, kind, m // 4, lax.rem(m, 4))
                flipped = jnp.where(rows[:, 88:89] == col, 1.0, 0.0).astype(bf16)
                pick[kind, m] = lax.dot_general(eye, flipped, NT, preferred_element_type=f32).astype(bf16)
                return 0

            lax.fori_loop(0, 16, one, 0, unroll=4)
        densify(8, 8, 0)
        start(c_x2())

    def counts_3():
        wait(c_x2())
        c2[0] = b1d[8, y]
        start(c_x3())

    def counts_4():
        wait(c_x3())
        total = jnp.zeros((64, LANES), f32)
        w0, w1 = total, total
        for kz in range(4):
            for ky in range(4):
                mm = c2[ky, z] if kz == 0 else c3[kz - 1, ky]
                n = 8 * (kz * 4 + ky)
                total = total + mm
                a = jnp.where(lane < 8, mm, 0.0)
                b = jnp.where((lane >= 80) & (lane < 88), mm, 0.0)
                w0 = w0 + (pltpu.roll(a, n, 1) if n else a)
                w1 = w1 + pltpu.roll(b, (n + 48) % 128, 1)
        offs = jnp.where((lane >= 8) & (lane < 72), total, 0.0)
        hits = jnp.sum(offs, axis=1, keepdims=True)
        inv[...] = jnp.broadcast_to(1.0 / (hits + 1.0), (64, LANES))
        wide = jnp.concatenate([w0, w1, pltpu.roll(offs, 120, 1)], axis=1)
        upper, lower = split(wide)
        left = jnp.concatenate([upper, lower], axis=0)
        for h in range(4):
            r1, r2 = split(r_ref[:, h * 256 : h * 256 + 256])
            both = jnp.concatenate([r1, r2], axis=1)
            out = lax.dot_general(left, jnp.concatenate([both, both], axis=0), TN, preferred_element_type=f32)
            u = out[:, 0:256] + out[:, 256:]
            us[:, :, :, :, h * 256 : h * 256 + 256] = u[0:256].reshape(2, 4, 4, 8, 256)
            uoff[:, h * 256 : h * 256 + 256] = u[256:320]
        start(u_core())

    def counts_5():
        wait(u_core())
        us[0] = us[0] + e0[...]
        start(u_y())

    def counts_6():
        wait(u_y())
        v2[...] = us[0, :, 0] + e1[0] + e1[1] + e1[2]
        start(u_z())

    def counts_7():
        wait(u_z())

    def w0(i):
        wait(x0(i))
        start(x1(i, KINDS[i], i))

    def w1(i):
        wait(x1(i, KINDS[i], i))
        densify(i, i, KINDS[i])
        start(x2(i, KINDS[i]))

    def w2(i):
        wait(x2(i, KINDS[i]))
        b2d[i] = b1d[i, me[SECOND[KINDS[i]]]] + b2[i, 0] + b2[i, 1] + b2[i, 2]
        start(x3(i, KINDS[i]))

    def w3(i):
        wait(x3(i, KINDS[i]))
        total = b2d[i, me[THIRD[KINDS[i]]]] + b3[i, 0] + b3[i, 1] + b3[i, 2]
        cols = slice(i * LANES, (i + 1) * LANES)
        rnew[:, cols] = (r_ref[:, cols] + total) * inv[...]

    mid = {0: [counts_1], 1: [lambda: w0(0)], 2: [lambda: w0(1), counts_3], 3: [lambda: w0(2), counts_4],
           4: [lambda: w0(3), counts_5], 5: [lambda: w0(4), counts_6], 6: [lambda: w0(5), counts_7], 7: [lambda: w0(6)]}
    end = {1: [counts_2], 3: [lambda: w1(0)], 4: [lambda: w1(1)], 5: [lambda: w1(2), lambda: w2(0)],
           6: [lambda: w1(3), lambda: w2(1)], 7: [lambda: w1(4), lambda: w2(2), lambda: w3(0)]}

    def chunk(i, _):
        at_lane = pl.multiple_of(i * LANES, LANES)
        chunk_table(i, range(0, NS, 16), cb, sb, table)
        for r in range(0, NS, 256):
            spec = jnp.dot(tr[r : r + 256, :], table[...], preferred_element_type=f32)
            re, im = spec[:, 0:LANES], spec[:, LANES:]
            amp = 0.5 * jnp.log(re * re + im * im + 0.01)
            upper, lower = split(amp)
            low[r : r + 256, 0:LANES] = upper
            low[r : r + 256, LANES:] = lower
        terms = jnp.concatenate([s_ref[:, pl.ds(at_lane, LANES)], o_ref[:, pl.ds(at_lane, LANES)]], axis=0)
        upper, lower = split(-terms)
        for r in (NS, NS + LANES):
            low[r : r + 72, 0:LANES] = upper
            low[r : r + 72, LANES:] = lower
        for n, todo in mid.items():
            @pl.when(i == n)
            def _(todo=todo):
                for f in todo:
                    f()
        for half in (0, 1):
            out = jnp.dot(hot[half * 512 : half * 512 + 512, :], low[...], preferred_element_type=f32)
            grid[i, 2 * half] = (out[:, 0:LANES] + out[:, LANES:]).reshape(4, 4, 4, 8, LANES)
        out = jnp.dot(hot[1024:ROWS, :], low[...], preferred_element_type=f32)
        extra[:, pl.ds(at_lane, LANES)] = (out[:, 0:LANES] + out[:, LANES:])[0:72]
        for n in range(8):
            @pl.when(i == n)
            def _(n=n):
                start(x0(n))
                for f in end.get(n, []):
                    f()
        return 0

    lax.fori_loop(0, 8, chunk, 0)

    ex[x, :, 0:1024] = extra[0:8, 0:1024] - (v2[0] + e2[0] + e2[1] + e2[2])
    ex[x, :, 1024:WIDE] = extra[0:8, 1024:WIDE]
    start(src_x())
    off[:, :, :, 0:1024] = (extra[8:72, 0:1024] - uoff[...]).reshape(2, 4, 8, 1024)
    off[:, :, :, 1024:WIDE] = extra[8:72, 1024:WIDE].reshape(2, 4, 8, LANES)
    start(off_core())
    w0(7)
    wait(off_core())
    ho[...] = off[c] + eo[...]
    start(off_x())
    w1(5)
    w2(3)
    w3(1)
    wait(off_x())
    eh2[y] = ho[x] + eh[0] + eh[1] + eh[2]
    start(off_y())
    w1(6)
    w2(4)
    w3(2)
    wait(off_y())
    eh3[z] = eh2[0] + eh2[1] + eh2[2] + eh2[3]
    start(off_z())
    w1(7)
    w2(5)
    w3(3)
    wait(off_z())
    fa[c, x] = eh3[0] + eh3[1] + eh3[2] + eh3[3]
    start(off_all())
    w2(6)
    w3(4)
    w2(7)
    w3(5)
    wait(src_x())
    total = ex[0] + ex[1] + ex[2] + ex[3]
    snew[...] = s_ref[...] + total[:, 0:1024] / (total[:, 1024:1025] + 1.0)
    wait(off_all())
    total = fa[...].reshape(64, WIDE)
    onew[...] = o_ref[...] + total[:, 0:1024] / (total[:, 1024:1025] + 1.0)
    w3(6)
    w3(7)


def local(traces, trace_source, trace_offset, trace_slot, request_list, src, rcv, off):
    f32, bf16 = jnp.float32, jnp.bfloat16
    vmem = pl.BlockSpec(memory_space=pltpu.VMEM)
    dma = pltpu.SemaphoreType.DMA
    scratch = [
        pltpu.VMEM((NS, NS), bf16),
        pltpu.VMEM((ROWS, NS + 256), bf16),
        pltpu.VMEM((NS, 256), bf16),
        pltpu.VMEM((NS, LANES), f32),
        pltpu.VMEM((NS, LANES), f32),
        pltpu.VMEM((NS + 256, 256), bf16),
        pltpu.VMEM((72, WIDE), f32),
        pltpu.VMEM((9, 3, 4, 4, 4, 8, LANES), f32),
        pltpu.VMEM((11, 3, 2, 4, 4, 8, LANES), f32),
        pltpu.VMEM((9, 4, 4, 64, LANES), f32),
        pltpu.VMEM((8, 3, 4, 64, LANES), f32),
        pltpu.VMEM((8, 4, 64, LANES), f32),
        pltpu.VMEM((8, 3, 64, LANES), f32),
        pltpu.VMEM((3, 16, 64, 64), bf16),
        pltpu.VMEM((4, 4, 64, LANES), f32),
        pltpu.VMEM((3, 4, 64, LANES), f32),
        pltpu.VMEM((2, 4, 4, 8, 1024), f32),
        pltpu.VMEM((4, 4, 8, 1024), f32),
        pltpu.VMEM((3, 4, 8, 1024), f32),
        pltpu.VMEM((4, 8, 1024), f32),
        pltpu.VMEM((3, 8, 1024), f32),
        pltpu.VMEM((64, 1024), f32),
        pltpu.VMEM((4, 8, WIDE), f32),
        pltpu.VMEM((2, 4, 8, WIDE), f32),
        pltpu.VMEM((4, 8, WIDE), f32),
        pltpu.VMEM((4, 8, WIDE), f32),
        pltpu.VMEM((3, 8, WIDE), f32),
        pltpu.VMEM((4, 8, WIDE), f32),
        pltpu.VMEM((4, 8, WIDE), f32),
        pltpu.VMEM((2, 4, 8, WIDE), f32),
        pltpu.VMEM((64, LANES), f32),
        dma,
        dma((9,)), dma((9,)), dma((11, 3)), dma((11, 3)), dma((9, 3)), dma((9, 3)), dma((9, 3)), dma((9, 3)),
        dma((7,)), dma((7,)), dma((17,)), dma((17,)), dma((3,)), dma((3,)),
    ]
    return pl.pallas_call(
        kernel,
        out_shape=(
            jax.ShapeDtypeStruct(src.shape, f32),
            jax.ShapeDtypeStruct(rcv.shape, f32),
            jax.ShapeDtypeStruct(off.shape, f32),
        ),
        in_specs=[pl.BlockSpec(memory_space=pl.ANY)] + [vmem] * 7,
        out_specs=(vmem, vmem, vmem),
        scratch_shapes=scratch,
        compiler_params=pltpu.CompilerParams(vmem_limit_bytes=58 << 20, collective_id=0, has_side_effects=True),
        name="update",
    )(
        traces,
        trace_slot.reshape(16, LANES),
        trace_source.reshape(16, LANES),
        trace_offset.reshape(16, LANES),
        request_list.reshape(128, 8).T,
        src,
        rcv,
        off,
    )


def solution(mesh):
    every = P(("src", "rcv"))
    return jax.shard_map(
        local,
        mesh=mesh,
        in_specs=(P(("src", "rcv"), None), every, every, every, P(("src", "rcv"), None, None), P("src", None), P(("src", "rcv"), None), P()),
        out_specs=(P("src", None), P(("src", "rcv"), None), P()),
        check_vma=False,
    )
```

```python
import math

import jax
import jax.numpy as jnp
from jax import lax
from jax.experimental import pallas as pl
from jax.experimental.pallas import tpu as pltpu
from jax.sharding import PartitionSpec as P

NS = 2048
LANES = 128
ROWS = 1152
WIDE = 1024 + LANES
MESH = pl.DeviceIdType.MESH
KINDS = ((0, 1, 2, 0, 1, 2, 0, 1), (1, 2, 0, 1, 2, 0, 1, 2))
SECOND = ("y", "z", "x")
THIRD = ("z", "x", "y")
TN = (((0,), (0,)), ((), ()))
STEP = 2.0 * math.pi / NS
NT = (((1,), (1,)), ((), ()))


def trig_base(cb, sb):
    row = lax.broadcasted_iota(jnp.int32, (128, LANES), 0)
    col = lax.broadcasted_iota(jnp.int32, (128, LANES), 1)
    far = ((row * 16 * col) % NS).astype(jnp.float32) * STEP
    far_c, far_s = jnp.cos(far), jnp.sin(far)
    wide = (row * 16).astype(jnp.float32) * STEP
    wide_c, wide_s = jnp.cos(wide), jnp.sin(wide)
    row = lax.broadcasted_iota(jnp.int32, (16, LANES), 0)
    col = lax.broadcasted_iota(jnp.int32, (16, LANES), 1)
    near = ((row * col) % NS).astype(jnp.float32) * STEP
    near_c, near_s = jnp.cos(near), jnp.sin(near)
    half = (row.astype(jnp.float32) + 0.5) * STEP
    half_c, half_s = jnp.cos(half), jnp.sin(half)
    for b in range(128):
        fc, fs = far_c[b : b + 1], far_s[b : b + 1]
        wc, ws = wide_c[b : b + 1], wide_s[b : b + 1]
        taper = (0.5 - 0.5 * (wc * half_c - ws * half_s)) * (1.0 / math.sqrt(NS))
        cb[16 * b : 16 * b + 16, :] = taper * (fc * near_c - fs * near_s)
        sb[16 * b : 16 * b + 16, :] = taper * (fs * near_c + fc * near_s)


def chunk_table(c, rows, cb, sb, table):
    n = lax.broadcasted_iota(jnp.int32, (16, LANES), 0)
    turn = ((n * c) % 16).astype(jnp.float32) * (2.0 * math.pi / 16.0)
    tc, ts = jnp.cos(turn), jnp.sin(turn)
    for r in rows:
        bc, bs = cb[r : r + 16, :], sb[r : r + 16, :]
        table[r : r + 16, 0:LANES] = (bc * tc - bs * ts).astype(jnp.bfloat16)
        table[r : r + 16, LANES : 2 * LANES] = (-(bs * tc + bc * ts)).astype(jnp.bfloat16)


def split(x):
    upper = x.astype(jnp.bfloat16)
    return upper, (x - upper.astype(jnp.float32)).astype(jnp.bfloat16)


def kernel(
    tr_hbm, slot_ref, src_ref, off_ref, list_ref, s_ref, r_ref, o_ref,
    snew, rnew, onew,
    tr, hot, table, cb, sb, low, extra,
    grid, b1, b1d, b2, b2d, b3, pick,
    c2, comb, c3, us, e0, e1, v2, e2, uoff, own_list, far_list,
    ex, off, eo, ho, eh, eh2, eh3, fa, inv,
    tr_sem, s0s, s0r, s1s, s1r, s2s, s2r, s3s, s3r, us_s, us_r, os_s, os_r, xs_s, xs_r, ls_s, ls_r,
):
    f32, bf16 = jnp.float32, jnp.bfloat16
    group, x = lax.axis_index("src"), lax.axis_index("rcv")
    c, z, y = lax.rem(group, 2), lax.rem(group // 2, 4), group // 8
    me = {"x": x, "y": y, "z": z}

    def at(ax, k, flip=False):
        p = dict(me)
        if ax:
            p[ax] = lax.rem(p[ax] + k, 4)
        core = 1 - c if flip else c
        return ((p["y"] * 4 + p["z"]) * 2 + core, p["x"])

    def step(ax, k):
        return lax.rem(me[ax] + k, 4)

    twin = at(None, 0, True)
    peers = [twin] + [at(ax, k) for ax in "xyz" for k in (1, 2, 3)] + [at("x", k, True) for k in (1, 2, 3)]
    barrier = pltpu.get_barrier_semaphore()
    for p in peers:
        pl.semaphore_signal(barrier, inc=1, device_id=p, device_id_type=MESH)

    load = pltpu.make_async_copy(tr_hbm, tr, tr_sem)
    load.start()

    def rc(a, b, ss, rs, dev):
        return pltpu.make_async_remote_copy(
            src_ref=a, dst_ref=b, send_sem=ss, recv_sem=rs, device_id=dev, device_id_type=MESH
        )

    def start(copies):
        for cp in copies:
            cp.start()

    def wait(copies):
        for cp in copies:
            cp.wait()

    def x0(i):
        return [rc(grid.at[i, 2], grid.at[i, 1], s0s.at[i], s0r.at[i], twin)]

    def x1(i, kind, n):
        out = []
        for k in (1, 2, 3):
            j = step("xyz"[kind], k)
            part = (grid.at[i, 0:2, :, :, j], grid.at[i, 0:2, j], grid.at[i, 0:2, :, j])[kind]
            out.append(rc(part, b1.at[n, k - 1], s1s.at[n, k - 1], s1r.at[n, k - 1], at("xyz"[kind], k)))
        return out

    def x2(i, kind):
        ax = SECOND[kind]
        return [
            rc(b1d.at[i, step(ax, k)], b2.at[i, k - 1], s2s.at[i, k - 1], s2r.at[i, k - 1], at(ax, k))
            for k in (1, 2, 3)
        ]

    def x3(i, kind):
        ax = THIRD[kind]
        return [
            rc(b2d.at[i, step(ax, k)], b3.at[i, k - 1], s3s.at[i, k - 1], s3r.at[i, k - 1], at(ax, k))
            for k in (1, 2, 3)
        ]

    def c_x2(a):
        return [rc(b1d.at[8, step(a, k)], c2.at[k], s2s.at[8, k - 1], s2r.at[8, k - 1], at(a, k)) for k in (1, 2, 3)]

    def c_x3(b):
        return [rc(comb.at[step(b, k)], c3.at[k - 1], s3s.at[8, k - 1], s3r.at[8, k - 1], at(b, k)) for k in (1, 2, 3)]

    def list_0():
        return [rc(own_list.at[0], own_list.at[1], ls_s.at[9], ls_r.at[9], twin)]

    def list_1():
        return [
            rc(own_list, far_list.at[n, k - 1], ls_s.at[3 * n + k - 1], ls_r.at[3 * n + k - 1], at(ax, k))
            for n, ax in enumerate("xyz")
            for k in (1, 2, 3)
        ]

    def u_core():
        return [rc(us.at[:, :, 1], e0, us_s.at[0], us_r.at[0], twin)]

    def u_near(a):
        return [rc(us.at[:, k, 0], e1.at[k - 1], us_s.at[k], us_r.at[k], at(a, 4 - k)) for k in (1, 2, 3)]

    def u_far(b):
        return [rc(v2.at[k], e2.at[k - 1], us_s.at[3 + k], us_r.at[3 + k], at(b, 4 - k)) for k in (1, 2, 3)]

    def src_x():
        return [rc(ex.at[x], ex.at[x], xs_s.at[k - 1], xs_r.at[k - 1], at("x", k)) for k in (1, 2, 3)]

    def off_core():
        return [rc(off.at[1 - c], eo, os_s.at[0], os_r.at[0], twin)]

    def off_x():
        return [rc(ho.at[step("x", k)], eh.at[k - 1], os_s.at[k], os_r.at[k], at("x", k)) for k in (1, 2, 3)]

    def off_y():
        return [rc(eh2.at[y], eh2.at[y], os_s.at[3 + k], os_r.at[3 + k], at("y", k)) for k in (1, 2, 3)]

    def off_z():
        return [rc(eh3.at[z], eh3.at[z], os_s.at[6 + k], os_r.at[6 + k], at("z", k)) for k in (1, 2, 3)]

    def off_all():
        to = [at("x", k) for k in (1, 2, 3)] + [twin] + [at("x", k, True) for k in (1, 2, 3)]
        return [rc(fa.at[c, x], fa.at[c, x], os_s.at[10 + n], os_r.at[10 + n], d) for n, d in enumerate(to)]

    s = slot_ref[...]
    row_of = (
        (((s >> 5) & 1) ^ c) * 512 + (s >> 8) * 128 + ((s >> 6) & 3) * 32 + ((s >> 3) & 3) * 8 + (s & 7)
    )
    first = src_ref[...] - group * 8 + 1024
    second = off_ref[...] + 1032

    def hot_rows(i, _):
        r = pl.multiple_of(i * 32, 32)
        row = lax.broadcasted_iota(jnp.int32, (32, LANES), 0) + r
        for b in range(16):
            hit = row == row_of[b : b + 1, :]
            hot[pl.ds(r, 32), b * LANES : (b + 1) * LANES] = jnp.where(hit, 1.0, 0.0).astype(bf16)
        return 0

    lax.fori_loop(0, 32, hot_rows, 0)
    for r in range(1024, ROWS, 32):
        row = lax.broadcasted_iota(jnp.int32, (32, LANES), 0) + r
        for b in range(16):
            hit = (row == first[b : b + 1, :]) | (row == second[b : b + 1, :])
            hot[r : r + 32, b * LANES : (b + 1) * LANES] = jnp.where(hit, 1.0, 0.0).astype(bf16)

    cnt = lax.dot_general(hot[:, 0:NS], hot[1024:ROWS, 0:NS], NT, preferred_element_type=f32)
    upper, lower = split(cnt)
    hot[:, NS : NS + LANES] = upper
    hot[:, NS + LANES : NS + 2 * LANES] = lower
    low[NS + 72 : NS + 128, :] = jnp.zeros((56, 2 * LANES), bf16)
    low[NS + 200 : NS + 256, :] = jnp.zeros((56, 2 * LANES), bf16)
    lane = lax.broadcasted_iota(jnp.int32, (1, LANES), 1)
    count_s = jnp.sum(jnp.where((lane >= 8) & (lane < 72), cnt[1024:1032], 0.0), axis=1, keepdims=True)
    count_o = jnp.sum(jnp.where(lane < 8, cnt[1032:1096], 0.0), axis=1, keepdims=True)
    extra[0:8, 1024:WIDE] = jnp.broadcast_to(count_s, (8, LANES))
    extra[8:72, 1024:WIDE] = jnp.broadcast_to(count_o, (64, LANES))

    grid[8, 0] = cnt[0:512].reshape(4, 4, 4, 8, LANES)
    far = cnt[512:1024]
    far = jnp.where((lane >= 80) & (lane < 88), pltpu.roll(far, 80, 1), jnp.where(lane < 8, 0.0, far))
    grid[8, 2] = far.reshape(4, 4, 4, 8, LANES)
    own_list[0] = list_ref[...].astype(f32)

    pl.semaphore_wait(barrier, len(peers))
    start(list_0())
    start(x0(8))
    trig_base(cb, sb)
    load.wait()

    def rows64(i, n, kind, p, q):
        own = (
            grid[i, 0:2, p, q, x] if kind == 0 else grid[i, 0:2, y, p, q] if kind == 1 else grid[i, 0:2, p, z, q]
        )
        return jnp.concatenate([own.reshape(16, LANES), b1[n, :, :, p, q].reshape(48, LANES)], axis=0)

    def densify(i, n, kind, swap=False):
        def one(m, _):
            p, q = m // 4, lax.rem(m, 4)
            upper, lower = split(rows64(i, n, kind, p, q))
            both = jnp.concatenate([upper, lower], axis=1)
            out = jnp.dot(pick[kind, m], both, preferred_element_type=f32)
            total = out[:, 0:LANES] + out[:, LANES:]
            if kind == 2 or swap:
                b1d[i, q, p] = total
            else:
                b1d[i, p, q] = total
            return 0

        lax.fori_loop(0, 16, one, 0, unroll=4)

    def counts_1():
        wait(list_0())
        start(list_1())
        wait(x0(8))
        start(x1(8, 0, 8))

    def lists():
        wait(list_1())
        row = lax.broadcasted_iota(jnp.int32, (1024, LANES), 0)
        col = lax.broadcasted_iota(jnp.int32, (1024, LANES), 1)
        p, q = row >> 8, (row >> 6) & 3
        want = (lax.broadcasted_iota(jnp.int32, (1024, 64), 0) & 63).astype(f32)
        for kind in range(3):
            py, pz, px = ((p, q, x), (y, p, q), (p, z, q))[kind]
            owner = ((py * 4 + pz) * 2 + c) * 4 + px
            which = jnp.where(col == owner, 1.0, 0.0).astype(bf16)
            rows = jnp.concatenate([own_list[...].reshape(16, LANES), far_list[kind].reshape(48, LANES)], axis=0)
            named = lax.dot_general(which, rows.astype(bf16), NT, preferred_element_type=f32)
            pick[kind] = jnp.where(named == want, 1.0, 0.0).astype(bf16).reshape(16, 64, 64)

    def by_core(f):
        for core, axes in enumerate((("y", "z"), ("z", "y"))):
            @pl.when(c == core)
            def _(axes=axes):
                f(*axes)

    def counts_2():
        wait(x1(8, 0, 8))

        def go(a, b):
            densify(8, 8, 0, swap=a == "z")
            start(c_x2(a))

        by_core(go)

    def counts_3():
        def go(a, b):
            wait(c_x2(a))
            c2[0] = b1d[8, me[a]]
            total = jnp.zeros((256, LANES), f32)
            for k in range(4):
                mm = c2[k].reshape(256, LANES)
                total = total + pltpu.roll(jnp.where((lane >= 8) & (lane < 72), mm, 0.0), 120, 1)
                total = total + pltpu.roll(jnp.where(lane < 8, mm, 0.0), 64 + 16 * k, 1)
                moved = (16 * k + 120) % 128
                one = jnp.where((lane >= 80) & (lane < 88), mm, 0.0)
                total = total + (pltpu.roll(one, moved, 1) if moved else one)
            comb[...] = total.reshape(4, 64, LANES)
            start(c_x3(b))

        by_core(go)

    def counts_4():
        by_core(lambda a, b: wait(c_x3(b)))
        parts = [comb[jnp.where(c == 0, z, y)], c3[0], c3[1], c3[2]]
        offs = jnp.where(lane < 64, parts[0] + parts[1] + parts[2] + parts[3], 0.0)
        hits = jnp.sum(offs, axis=1, keepdims=True)
        inv[...] = jnp.broadcast_to(1.0 / (hits + 1.0), (64, LANES))
        high = [jnp.where(lane >= 64, v, 0.0) for v in parts]
        wide = jnp.concatenate([pltpu.roll(high[0], 64, 1) + high[1], pltpu.roll(high[2], 64, 1) + high[3], offs], axis=1)
        upper, lower = split(wide)
        left = jnp.concatenate([upper, lower], axis=0)
        for h in range(4):
            r1, r2 = split(r_ref[:, h * 256 : h * 256 + 256])
            both = jnp.concatenate([r1, r2], axis=1)
            out = lax.dot_general(left, jnp.concatenate([both, both], axis=0), TN, preferred_element_type=f32)
            u = out[:, 0:256] + out[:, 256:]
            us[:, :, :, :, h * 256 : h * 256 + 256] = u[0:256].reshape(4, 4, 2, 8, 256)
            uoff[:, h * 256 : h * 256 + 256] = u[256:320]
        start(u_core())

    def counts_5():
        wait(u_core())
        for p in range(4):
            for q in range(4):
                us[p, q, 0] = us[p, q, 0] + e0[q, p]
        by_core(lambda a, b: start(u_near(a)))

    def counts_6():
        by_core(lambda a, b: wait(u_near(a)))
        v2[...] = us[:, 0, 0] + e1[0] + e1[1] + e1[2]
        by_core(lambda a, b: start(u_far(b)))

    def counts_7():
        by_core(lambda a, b: wait(u_far(b)))
        ex[x, :, 0:1024] = extra[0:8, 0:1024] - (v2[0] + e2[0] + e2[1] + e2[2])
        ex[x, :, 1024:WIDE] = extra[0:8, 1024:WIDE]
        start(src_x())

    def each_core(i, f):
        for core in (0, 1):
            @pl.when(c == core)
            def _(kind=KINDS[core][i]):
                f(kind)

    def w0(i):
        wait(x0(i))
        each_core(i, lambda kind: start(x1(i, kind, i)))

    def w1(i):
        def go(kind):
            wait(x1(i, kind, i))
            densify(i, i, kind)
            start(x2(i, kind))

        each_core(i, go)

    def w2(i):
        def go(kind):
            wait(x2(i, kind))
            b2d[i] = b1d[i, me[SECOND[kind]]] + b2[i, 0] + b2[i, 1] + b2[i, 2]
            start(x3(i, kind))

        each_core(i, go)

    def w3(i):
        def go(kind):
            wait(x3(i, kind))
            total = b2d[i, me[THIRD[kind]]] + b3[i, 0] + b3[i, 1] + b3[i, 2]
            cols = slice(i * LANES, (i + 1) * LANES)
            rnew[:, cols] = (r_ref[:, cols] + total) * inv[...]

        each_core(i, go)

    def later(f, n):
        return lambda: f(n)

    first = {2: [counts_2], 4: [counts_3], 5: [counts_4], 6: [counts_5]}
    mid = {
        0: [counts_1], 1: [later(w0, 0)], 2: [later(w0, 1)], 3: [later(w0, 2)], 4: [later(w0, 3), later(w2, 0)],
        5: [later(w0, 4), later(w2, 1)], 6: [later(w0, 5), later(w2, 2)], 7: [later(w0, 6), later(w2, 3), counts_6],
    }
    end = {
        1: [lists], 2: [later(w1, 0)], 3: [later(w1, 1)], 4: [later(w1, 2)], 5: [later(w1, 3)],
        6: [later(w1, 4), later(w3, 0)], 7: [later(w1, 5), later(w3, 1)],
    }

    def point(i, table_of):
        for n, todo in table_of.items():
            @pl.when(i == n)
            def _(todo=todo):
                for f in todo:
                    f()

    def chunk(i, _):
        at_lane = pl.multiple_of(i * LANES, LANES)
        point(i, first)
        chunk_table(i, range(0, NS, 16), cb, sb, table)
        for r in range(0, NS, 256):
            spec = jnp.dot(tr[r : r + 256, :], table[...], preferred_element_type=f32)
            re, im = spec[:, 0:LANES], spec[:, LANES:]
            amp = 0.5 * jnp.log(re * re + im * im + 0.01)
            upper, lower = split(amp)
            low[r : r + 256, 0:LANES] = upper
            low[r : r + 256, LANES:] = lower
        terms = jnp.concatenate([s_ref[:, pl.ds(at_lane, LANES)], o_ref[:, pl.ds(at_lane, LANES)]], axis=0)
        upper, lower = split(-terms)
        for r in (NS, NS + LANES):
            low[r : r + 72, 0:LANES] = upper
            low[r : r + 72, LANES:] = lower
        point(i, mid)
        for half in (0, 1):
            out = jnp.dot(hot[half * 512 : half * 512 + 512, :], low[...], preferred_element_type=f32)
            grid[i, 2 * half] = (out[:, 0:LANES] + out[:, LANES:]).reshape(4, 4, 4, 8, LANES)
        out = jnp.dot(hot[1024:ROWS, :], low[...], preferred_element_type=f32)
        extra[:, pl.ds(at_lane, LANES)] = (out[:, 0:LANES] + out[:, LANES:])[0:72]
        for n in range(8):
            @pl.when(i == n)
            def _(n=n):
                start(x0(n))
                for f in end.get(n, []):
                    f()
        return 0

    lax.fori_loop(0, 8, chunk, 0)

    off[:, :, :, 0:1024] = (extra[8:72, 0:1024] - uoff[...]).reshape(2, 4, 8, 1024)
    off[:, :, :, 1024:WIDE] = extra[8:72, 1024:WIDE].reshape(2, 4, 8, LANES)
    start(off_core())
    w2(4)
    w3(2)
    w0(7)
    wait(off_core())
    ho[...] = off[c] + eo[...]
    start(off_x())
    w3(3)
    w1(6)
    counts_7()
    wait(off_x())
    eh2[y] = ho[x] + eh[0] + eh[1] + eh[2]
    start(off_y())
    w2(5)
    wait(off_y())
    eh3[z] = eh2[0] + eh2[1] + eh2[2] + eh2[3]
    start(off_z())
    w1(7)
    w3(4)
    wait(off_z())
    fa[c, x] = eh3[0] + eh3[1] + eh3[2] + eh3[3]
    start(off_all())
    w2(6)
    w3(5)
    wait(src_x())
    total = ex[0] + ex[1] + ex[2] + ex[3]
    snew[...] = s_ref[...] + total[:, 0:1024] / (total[:, 1024:1025] + 1.0)
    w2(7)
    w3(6)
    wait(off_all())
    total = fa[...].reshape(64, WIDE)
    onew[...] = o_ref[...] + total[:, 0:1024] / (total[:, 1024:1025] + 1.0)
    w3(7)


def hand_over(a, b, d, oa, ob, od):
    oa[...] = a[...]
    ob[...] = b[...]
    od[...] = d[...]


def local(traces, trace_source, trace_offset, trace_slot, request_list, src, rcv, off):
    f32, bf16 = jnp.float32, jnp.bfloat16
    vmem = pl.BlockSpec(memory_space=pltpu.VMEM)
    dma = pltpu.SemaphoreType.DMA
    scratch = [
        pltpu.VMEM((NS, NS), bf16),
        pltpu.VMEM((ROWS, NS + 256), bf16),
        pltpu.VMEM((NS, 256), bf16),
        pltpu.VMEM((NS, LANES), f32),
        pltpu.VMEM((NS, LANES), f32),
        pltpu.VMEM((NS + 256, 256), bf16),
        pltpu.VMEM((72, WIDE), f32),
        pltpu.VMEM((9, 3, 4, 4, 4, 8, LANES), f32),
        pltpu.VMEM((9, 3, 2, 4, 4, 8, LANES), f32),
        pltpu.VMEM((9, 4, 4, 64, LANES), f32),
        pltpu.VMEM((8, 3, 4, 64, LANES), f32),
        pltpu.VMEM((8, 4, 64, LANES), f32),
        pltpu.VMEM((8, 3, 64, LANES), f32),
        pltpu.VMEM((3, 16, 64, 64), bf16),
        pltpu.VMEM((4, 4, 64, LANES), f32),
        pltpu.VMEM((4, 64, LANES), f32),
        pltpu.VMEM((3, 64, LANES), f32),
        pltpu.VMEM((4, 4, 2, 8, 1024), f32),
        pltpu.VMEM((4, 4, 8, 1024), f32),
        pltpu.VMEM((3, 4, 8, 1024), f32),
        pltpu.VMEM((4, 8, 1024), f32),
        pltpu.VMEM((3, 8, 1024), f32),
        pltpu.VMEM((64, 1024), f32),
        pltpu.VMEM((2, 8, LANES), f32),
        pltpu.VMEM((3, 3, 2, 8, LANES), f32),
        pltpu.VMEM((4, 8, WIDE), f32),
        pltpu.VMEM((2, 4, 8, WIDE), f32),
        pltpu.VMEM((4, 8, WIDE), f32),
        pltpu.VMEM((4, 8, WIDE), f32),
        pltpu.VMEM((3, 8, WIDE), f32),
        pltpu.VMEM((4, 8, WIDE), f32),
        pltpu.VMEM((4, 8, WIDE), f32),
        pltpu.VMEM((2, 4, 8, WIDE), f32),
        pltpu.VMEM((64, LANES), f32),
        dma,
        dma((9,)), dma((9,)), dma((9, 3)), dma((9, 3)), dma((9, 3)), dma((9, 3)), dma((9, 3)), dma((9, 3)),
        dma((7,)), dma((7,)), dma((17,)), dma((17,)), dma((3,)), dma((3,)), dma((10,)), dma((10,)),
    ]
    shapes = tuple(jax.ShapeDtypeStruct(v.shape, f32) for v in (src, rcv, off))
    parts = pl.pallas_call(
        kernel,
        out_shape=shapes,
        in_specs=[pl.BlockSpec(memory_space=pl.ANY)] + [vmem] * 7,
        out_specs=(vmem, vmem, vmem),
        scratch_shapes=scratch,
        compiler_params=pltpu.CompilerParams(vmem_limit_bytes=58 << 20, collective_id=0, has_side_effects=True),
        name="update",
    )(
        traces,
        trace_slot.reshape(16, LANES),
        trace_source.reshape(16, LANES),
        trace_offset.reshape(16, LANES),
        request_list.reshape(128, 8).T,
        src,
        rcv,
        off,
    )
    return pl.pallas_call(
        hand_over,
        out_shape=shapes,
        in_specs=[vmem] * 3,
        out_specs=(vmem,) * 3,
        name="hand_over",
    )(*parts)


def solution(mesh):
    every = P(("src", "rcv"))
    return jax.shard_map(
        local,
        mesh=mesh,
        in_specs=(P(("src", "rcv"), None), every, every, every, P(("src", "rcv"), None, None), P("src", None), P(("src", "rcv"), None), P()),
        out_specs=(P("src", None), P(("src", "rcv"), None), P()),
        check_vma=False,
    )
```

```python
import math

import jax
import jax.numpy as jnp
from jax import lax
from jax.experimental import pallas as pl
from jax.experimental.pallas import tpu as pltpu
from jax.sharding import PartitionSpec as P

NS = 2048
LANES = 128
ROWS = 1152
WIDE = 1024 + LANES
MESH = pl.DeviceIdType.MESH
KINDS = ((0, 1, 2, 0, 1, 2, 0, 1), (1, 2, 0, 1, 2, 0, 1, 2))
SECOND = ("y", "z", "x")
THIRD = ("z", "x", "y")
TN = (((0,), (0,)), ((), ()))
STEP = 2.0 * math.pi / NS
NT = (((1,), (1,)), ((), ()))


def trig_base(cb, sb):
    row = lax.broadcasted_iota(jnp.int32, (128, LANES), 0)
    col = lax.broadcasted_iota(jnp.int32, (128, LANES), 1)
    far = ((row * 16 * col) % NS).astype(jnp.float32) * STEP
    far_c, far_s = jnp.cos(far), jnp.sin(far)
    wide = (row * 16).astype(jnp.float32) * STEP
    wide_c, wide_s = jnp.cos(wide), jnp.sin(wide)
    row = lax.broadcasted_iota(jnp.int32, (16, LANES), 0)
    col = lax.broadcasted_iota(jnp.int32, (16, LANES), 1)
    near = ((row * col) % NS).astype(jnp.float32) * STEP
    near_c, near_s = jnp.cos(near), jnp.sin(near)
    half = (row.astype(jnp.float32) + 0.5) * STEP
    half_c, half_s = jnp.cos(half), jnp.sin(half)
    for b in range(128):
        fc, fs = far_c[b : b + 1], far_s[b : b + 1]
        wc, ws = wide_c[b : b + 1], wide_s[b : b + 1]
        taper = (0.5 - 0.5 * (wc * half_c - ws * half_s)) * (1.0 / math.sqrt(NS))
        cb[16 * b : 16 * b + 16, :] = taper * (fc * near_c - fs * near_s)
        sb[16 * b : 16 * b + 16, :] = taper * (fs * near_c + fc * near_s)


def chunk_table(c, rows, cb, sb, table):
    n = lax.broadcasted_iota(jnp.int32, (16, LANES), 0)
    turn = ((n * c) % 16).astype(jnp.float32) * (2.0 * math.pi / 16.0)
    tc, ts = jnp.cos(turn), jnp.sin(turn)
    for r in rows:
        bc, bs = cb[r : r + 16, :], sb[r : r + 16, :]
        table[r : r + 16, 0:LANES] = (bc * tc - bs * ts).astype(jnp.bfloat16)
        table[r : r + 16, LANES : 2 * LANES] = (-(bs * tc + bc * ts)).astype(jnp.bfloat16)


def split(x):
    upper = x.astype(jnp.bfloat16)
    return upper, (x - upper.astype(jnp.float32)).astype(jnp.bfloat16)


def kernel(
    tr_hbm, slot_ref, src_ref, off_ref, list_ref, s_ref, r_ref, o_ref,
    snew, rnew, onew,
    tr, hot, table, cb, sb, low, extra,
    grid, b1, b1d, b2, b2d, b3, pick,
    c2, comb, c3, us, e0, e1, v2, e2, uoff, own_list, far_list,
    ex, off, eo, ho, eh, eh2, eh3, fa, inv,
    tr_sem, s0s, s0r, s1s, s1r, s2s, s2r, s3s, s3r, us_s, us_r, os_s, os_r, xs_s, xs_r, ls_s, ls_r,
):
    f32, bf16 = jnp.float32, jnp.bfloat16
    group, x = lax.axis_index("src"), lax.axis_index("rcv")
    c, z, y = lax.rem(group, 2), lax.rem(group // 2, 4), group // 8
    me = {"x": x, "y": y, "z": z}

    def at(ax, k, flip=False):
        p = dict(me)
        if ax:
            p[ax] = lax.rem(p[ax] + k, 4)
        core = 1 - c if flip else c
        return ((p["y"] * 4 + p["z"]) * 2 + core, p["x"])

    def step(ax, k):
        return lax.rem(me[ax] + k, 4)

    twin = at(None, 0, True)
    peers = [twin] + [at(ax, k) for ax in "xyz" for k in (1, 2, 3)] + [at("x", k, True) for k in (1, 2, 3)]
    barrier = pltpu.get_barrier_semaphore()
    for p in peers:
        pl.semaphore_signal(barrier, inc=1, device_id=p, device_id_type=MESH)

    load = pltpu.make_async_copy(tr_hbm, tr, tr_sem)
    load.start()

    def rc(a, b, ss, rs, dev):
        return pltpu.make_async_remote_copy(
            src_ref=a, dst_ref=b, send_sem=ss, recv_sem=rs, device_id=dev, device_id_type=MESH
        )

    def start(copies):
        for cp in copies:
            cp.start()

    def wait(copies):
        for cp in copies:
            cp.wait()

    def x0(i):
        return [rc(grid.at[i, 2], grid.at[i, 1], s0s.at[i], s0r.at[i], twin)]

    def x1(i, kind, n):
        out = []
        for k in (1, 2, 3):
            j = step("xyz"[kind], k)
            part = (grid.at[i, 0:2, :, :, j], grid.at[i, 0:2, j], grid.at[i, 0:2, :, j])[kind]
            out.append(rc(part, b1.at[n, k - 1], s1s.at[n, k - 1], s1r.at[n, k - 1], at("xyz"[kind], k)))
        return out

    def x2(i, kind):
        ax = SECOND[kind]
        return [
            rc(b1d.at[i, step(ax, k)], b2.at[i, k - 1], s2s.at[i, k - 1], s2r.at[i, k - 1], at(ax, k))
            for k in (1, 2, 3)
        ]

    def x3(i, kind):
        ax = THIRD[kind]
        return [
            rc(b2d.at[i, step(ax, k)], b3.at[i, k - 1], s3s.at[i, k - 1], s3r.at[i, k - 1], at(ax, k))
            for k in (1, 2, 3)
        ]

    def c_x2(a):
        return [rc(b1d.at[8, step(a, k)], c2.at[k], s2s.at[8, k - 1], s2r.at[8, k - 1], at(a, k)) for k in (1, 2, 3)]

    def c_x3(b):
        return [rc(comb.at[step(b, k)], c3.at[k - 1], s3s.at[8, k - 1], s3r.at[8, k - 1], at(b, k)) for k in (1, 2, 3)]

    def list_0():
        return [rc(own_list.at[0], own_list.at[1], ls_s.at[9], ls_r.at[9], twin)]

    def list_1():
        return [
            rc(own_list, far_list.at[n, k - 1], ls_s.at[3 * n + k - 1], ls_r.at[3 * n + k - 1], at(ax, k))
            for n, ax in enumerate("xyz")
            for k in (1, 2, 3)
        ]

    def u_core():
        return [rc(us.at[:, :, 1], e0, us_s.at[0], us_r.at[0], twin)]

    def u_near(a):
        return [rc(us.at[:, k, 0], e1.at[k - 1], us_s.at[k], us_r.at[k], at(a, 4 - k)) for k in (1, 2, 3)]

    def u_far(b):
        return [rc(v2.at[k], e2.at[k - 1], us_s.at[3 + k], us_r.at[3 + k], at(b, 4 - k)) for k in (1, 2, 3)]

    def src_x():
        return [rc(ex.at[x], ex.at[x], xs_s.at[k - 1], xs_r.at[k - 1], at("x", k)) for k in (1, 2, 3)]

    def off_core():
        return [rc(off.at[1 - c], eo, os_s.at[0], os_r.at[0], twin)]

    def off_x():
        return [rc(ho.at[step("x", k)], eh.at[k - 1], os_s.at[k], os_r.at[k], at("x", k)) for k in (1, 2, 3)]

    def off_y():
        return [rc(eh2.at[y], eh2.at[y], os_s.at[3 + k], os_r.at[3 + k], at("y", k)) for k in (1, 2, 3)]

    def off_z():
        return [rc(eh3.at[z], eh3.at[z], os_s.at[6 + k], os_r.at[6 + k], at("z", k)) for k in (1, 2, 3)]

    def off_all():
        to = [at("x", k) for k in (1, 2, 3)] + [twin] + [at("x", k, True) for k in (1, 2, 3)]
        return [rc(fa.at[c, x], fa.at[c, x], os_s.at[10 + n], os_r.at[10 + n], d) for n, d in enumerate(to)]

    s = slot_ref[...]
    row_of = (
        (((s >> 5) & 1) ^ c) * 512 + (s >> 8) * 128 + ((s >> 6) & 3) * 32 + ((s >> 3) & 3) * 8 + (s & 7)
    )
    first = src_ref[...] - group * 8 + 1024
    second = off_ref[...] + 1032

    def hot_rows(i, _):
        r = pl.multiple_of(i * 32, 32)
        row = lax.broadcasted_iota(jnp.int32, (32, LANES), 0) + r
        for b in range(16):
            hit = row == row_of[b : b + 1, :]
            hot[pl.ds(r, 32), b * LANES : (b + 1) * LANES] = jnp.where(hit, 1.0, 0.0).astype(bf16)
        return 0

    lax.fori_loop(0, 32, hot_rows, 0)
    for r in range(1024, ROWS, 32):
        row = lax.broadcasted_iota(jnp.int32, (32, LANES), 0) + r
        for b in range(16):
            hit = (row == first[b : b + 1, :]) | (row == second[b : b + 1, :])
            hot[r : r + 32, b * LANES : (b + 1) * LANES] = jnp.where(hit, 1.0, 0.0).astype(bf16)

    cnt = lax.dot_general(hot[:, 0:NS], hot[1024:ROWS, 0:NS], NT, preferred_element_type=f32)
    upper, lower = split(cnt)
    hot[:, NS : NS + LANES] = upper
    hot[:, NS + LANES : NS + 2 * LANES] = lower
    low[NS + 72 : NS + 128, :] = jnp.zeros((56, 2 * LANES), bf16)
    low[NS + 200 : NS + 256, :] = jnp.zeros((56, 2 * LANES), bf16)
    lane = lax.broadcasted_iota(jnp.int32, (1, LANES), 1)
    count_s = jnp.sum(jnp.where((lane >= 8) & (lane < 72), cnt[1024:1032], 0.0), axis=1, keepdims=True)
    count_o = jnp.sum(jnp.where(lane < 8, cnt[1032:1096], 0.0), axis=1, keepdims=True)
    extra[0:8, 1024:WIDE] = jnp.broadcast_to(count_s, (8, LANES))
    extra[8:72, 1024:WIDE] = jnp.broadcast_to(count_o, (64, LANES))

    grid[8, 0] = cnt[0:512].reshape(4, 4, 4, 8, LANES)
    far = cnt[512:1024]
    far = jnp.where((lane >= 80) & (lane < 88), pltpu.roll(far, 80, 1), jnp.where(lane < 8, 0.0, far))
    grid[8, 2] = far.reshape(4, 4, 4, 8, LANES)
    own_list[0] = list_ref[...].astype(f32)

    pl.semaphore_wait(barrier, len(peers))
    start(list_0())
    start(x0(8))
    trig_base(cb, sb)
    load.wait()

    def rows64(i, n, kind, p, q):
        own = (
            grid[i, 0:2, p, q, x] if kind == 0 else grid[i, 0:2, y, p, q] if kind == 1 else grid[i, 0:2, p, z, q]
        )
        return jnp.concatenate([own.reshape(16, LANES), b1[n, :, :, p, q].reshape(48, LANES)], axis=0)

    def densify(i, n, kind, swap=False):
        def one(m, _):
            p, q = m // 4, lax.rem(m, 4)
            upper, lower = split(rows64(i, n, kind, p, q))
            both = jnp.concatenate([upper, lower], axis=1)
            out = jnp.dot(pick[kind, m], both, preferred_element_type=f32)
            total = out[:, 0:LANES] + out[:, LANES:]
            if kind == 2 or swap:
                b1d[i, q, p] = total
            else:
                b1d[i, p, q] = total
            return 0

        lax.fori_loop(0, 16, one, 0, unroll=4)

    def counts_1():
        wait(list_0())
        start(list_1())
        wait(x0(8))
        start(x1(8, 0, 8))

    def lists():
        wait(list_1())
        row = lax.broadcasted_iota(jnp.int32, (1024, LANES), 0)
        col = lax.broadcasted_iota(jnp.int32, (1024, LANES), 1)
        p, q = row >> 8, (row >> 6) & 3
        want = (lax.broadcasted_iota(jnp.int32, (1024, 64), 0) & 63).astype(f32)
        for kind in range(3):
            py, pz, px = ((p, q, x), (y, p, q), (p, z, q))[kind]
            owner = ((py * 4 + pz) * 2 + c) * 4 + px
            which = jnp.where(col == owner, 1.0, 0.0).astype(bf16)
            rows = jnp.concatenate([own_list[...].reshape(16, LANES), far_list[kind].reshape(48, LANES)], axis=0)
            named = lax.dot_general(which, rows.astype(bf16), NT, preferred_element_type=f32)
            pick[kind] = jnp.where(named == want, 1.0, 0.0).astype(bf16).reshape(16, 64, 64)

    def by_core(f):
        for core, axes in enumerate((("y", "z"), ("z", "y"))):
            @pl.when(c == core)
            def _(axes=axes):
                f(*axes)

    def counts_2():
        wait(x1(8, 0, 8))

        def go(a, b):
            densify(8, 8, 0, swap=a == "z")
            start(c_x2(a))

        by_core(go)

    def counts_3():
        def go(a, b):
            wait(c_x2(a))
            c2[0] = b1d[8, me[a]]
            total = jnp.zeros((256, LANES), f32)
            for k in range(4):
                mm = c2[k].reshape(256, LANES)
                total = total + pltpu.roll(jnp.where((lane >= 8) & (lane < 72), mm, 0.0), 120, 1)
                total = total + pltpu.roll(jnp.where(lane < 8, mm, 0.0), 64 + 16 * k, 1)
                moved = (16 * k + 120) % 128
                one = jnp.where((lane >= 80) & (lane < 88), mm, 0.0)
                total = total + (pltpu.roll(one, moved, 1) if moved else one)
            comb[...] = total.reshape(4, 64, LANES)
            start(c_x3(b))

        by_core(go)

    def counts_4():
        by_core(lambda a, b: wait(c_x3(b)))
        parts = [comb[jnp.where(c == 0, z, y)], c3[0], c3[1], c3[2]]
        offs = jnp.where(lane < 64, parts[0] + parts[1] + parts[2] + parts[3], 0.0)
        hits = jnp.sum(offs, axis=1, keepdims=True)
        inv[...] = jnp.broadcast_to(1.0 / (hits + 1.0), (64, LANES))
        high = [jnp.where(lane >= 64, v, 0.0) for v in parts]
        wide = jnp.concatenate([pltpu.roll(high[0], 64, 1) + high[1], pltpu.roll(high[2], 64, 1) + high[3], offs], axis=1)
        upper, lower = split(wide)
        left = jnp.concatenate([upper, lower], axis=0)
        for h in range(4):
            r1, r2 = split(r_ref[:, h * 256 : h * 256 + 256])
            both = jnp.concatenate([r1, r2], axis=1)
            out = lax.dot_general(left, jnp.concatenate([both, both], axis=0), TN, preferred_element_type=f32)
            u = out[:, 0:256] + out[:, 256:]
            us[:, :, :, :, h * 256 : h * 256 + 256] = u[0:256].reshape(4, 4, 2, 8, 256)
            uoff[:, h * 256 : h * 256 + 256] = u[256:320]
        start(u_core())

    def counts_5():
        wait(u_core())
        for p in range(4):
            for q in range(4):
                us[p, q, 0] = us[p, q, 0] + e0[q, p]
        by_core(lambda a, b: start(u_near(a)))

    def counts_6():
        by_core(lambda a, b: wait(u_near(a)))
        v2[...] = us[:, 0, 0] + e1[0] + e1[1] + e1[2]
        by_core(lambda a, b: start(u_far(b)))

    def counts_7():
        by_core(lambda a, b: wait(u_far(b)))
        ex[x, :, 0:1024] = extra[0:8, 0:1024] - (v2[0] + e2[0] + e2[1] + e2[2])
        ex[x, :, 1024:WIDE] = extra[0:8, 1024:WIDE]
        start(src_x())

    def each_core(i, f):
        for core in (0, 1):
            @pl.when(c == core)
            def _(kind=KINDS[core][i]):
                f(kind)

    def w0(i):
        wait(x0(i))
        each_core(i, lambda kind: start(x1(i, kind, i)))

    def w1(i):
        def go(kind):
            wait(x1(i, kind, i))
            densify(i, i, kind)
            start(x2(i, kind))

        each_core(i, go)

    def w2(i):
        def go(kind):
            wait(x2(i, kind))
            b2d[i] = b1d[i, me[SECOND[kind]]] + b2[i, 0] + b2[i, 1] + b2[i, 2]
            start(x3(i, kind))

        each_core(i, go)

    def w3(i):
        def go(kind):
            wait(x3(i, kind))
            total = b2d[i, me[THIRD[kind]]] + b3[i, 0] + b3[i, 1] + b3[i, 2]
            cols = slice(i * LANES, (i + 1) * LANES)
            rnew[:, cols] = (r_ref[:, cols] + total) * inv[...]

        each_core(i, go)

    def later(f, n):
        return lambda: f(n)

    first = {
        2: [lists],
        3: [later(w1, 0)],
        4: [later(w1, 1)],
        5: [later(w1, 2), later(w2, 0)],
        6: [later(w1, 3), later(w2, 1)],
        7: [later(w1, 4), later(w2, 2)],
    }
    mid = {
        0: [counts_1],
        1: [later(w0, 0)],
        2: [later(w0, 1)],
        3: [later(w0, 2)],
        4: [later(w0, 3)],
        5: [later(w0, 4)],
        6: [later(w0, 5), later(w3, 0)],
        7: [later(w0, 6), later(w3, 1)],
    }
    end = {
        2: [counts_2],
        4: [counts_3],
        5: [counts_4],
        6: [counts_5],
    }

    def point(i, table_of):
        for n, todo in table_of.items():
            @pl.when(i == n)
            def _(todo=todo):
                for f in todo:
                    f()

    def chunk(i, _):
        at_lane = pl.multiple_of(i * LANES, LANES)
        point(i, first)
        chunk_table(i, range(0, NS, 16), cb, sb, table)
        for r in range(0, NS, 256):
            spec = jnp.dot(tr[r : r + 256, :], table[...], preferred_element_type=f32)
            re, im = spec[:, 0:LANES], spec[:, LANES:]
            amp = 0.5 * jnp.log(re * re + im * im + 0.01)
            upper, lower = split(amp)
            low[r : r + 256, 0:LANES] = upper
            low[r : r + 256, LANES:] = lower
        terms = jnp.concatenate([s_ref[:, pl.ds(at_lane, LANES)], o_ref[:, pl.ds(at_lane, LANES)]], axis=0)
        upper, lower = split(-terms)
        for r in (NS, NS + LANES):
            low[r : r + 72, 0:LANES] = upper
            low[r : r + 72, LANES:] = lower
        point(i, mid)
        for half in (0, 1):
            out = jnp.dot(hot[half * 512 : half * 512 + 512, :], low[...], preferred_element_type=f32)
            grid[i, 2 * half] = (out[:, 0:LANES] + out[:, LANES:]).reshape(4, 4, 4, 8, LANES)
        out = jnp.dot(hot[1024:ROWS, :], low[...], preferred_element_type=f32)
        extra[:, pl.ds(at_lane, LANES)] = (out[:, 0:LANES] + out[:, LANES:])[0:72]
        for n in range(8):
            @pl.when(i == n)
            def _(n=n):
                start(x0(n))
                for f in end.get(n, []):
                    f()
        return 0

    lax.fori_loop(0, 8, chunk, 0)

    off[:, :, :, 0:1024] = (extra[8:72, 0:1024] - uoff[...]).reshape(2, 4, 8, 1024)
    off[:, :, :, 1024:WIDE] = extra[8:72, 1024:WIDE].reshape(2, 4, 8, LANES)
    start(off_core())
    w1(5)
    w2(3)
    counts_6()
    w0(7)
    w3(2)
    wait(off_core())
    ho[...] = off[c] + eo[...]
    start(off_x())
    w1(6)
    w2(4)
    w3(3)
    counts_7()
    wait(off_x())
    eh2[y] = ho[x] + eh[0] + eh[1] + eh[2]
    start(off_y())
    w1(7)
    w2(5)
    w3(4)
    wait(off_y())
    eh3[z] = eh2[0] + eh2[1] + eh2[2] + eh2[3]
    start(off_z())
    w2(6)
    w3(5)
    wait(off_z())
    fa[c, x] = eh3[0] + eh3[1] + eh3[2] + eh3[3]
    start(off_all())
    w2(7)
    w3(6)
    wait(off_all())
    total = fa[...].reshape(64, WIDE)
    onew[...] = o_ref[...] + total[:, 0:1024] / (total[:, 1024:1025] + 1.0)
    wait(src_x())
    total = ex[0] + ex[1] + ex[2] + ex[3]
    snew[...] = s_ref[...] + total[:, 0:1024] / (total[:, 1024:1025] + 1.0)
    w3(7)


def hand_over(a, b, d, oa, ob, od):
    oa[...] = a[...]
    ob[...] = b[...]
    od[...] = d[...]


def local(traces, trace_source, trace_offset, trace_slot, request_list, src, rcv, off):
    f32, bf16 = jnp.float32, jnp.bfloat16
    vmem = pl.BlockSpec(memory_space=pltpu.VMEM)
    dma = pltpu.SemaphoreType.DMA
    scratch = [
        pltpu.VMEM((NS, NS), bf16),
        pltpu.VMEM((ROWS, NS + 256), bf16),
        pltpu.VMEM((NS, 256), bf16),
        pltpu.VMEM((NS, LANES), f32),
        pltpu.VMEM((NS, LANES), f32),
        pltpu.VMEM((NS + 256, 256), bf16),
        pltpu.VMEM((72, WIDE), f32),
        pltpu.VMEM((9, 3, 4, 4, 4, 8, LANES), f32),
        pltpu.VMEM((9, 3, 2, 4, 4, 8, LANES), f32),
        pltpu.VMEM((9, 4, 4, 64, LANES), f32),
        pltpu.VMEM((8, 3, 4, 64, LANES), f32),
        pltpu.VMEM((8, 4, 64, LANES), f32),
        pltpu.VMEM((8, 3, 64, LANES), f32),
        pltpu.VMEM((3, 16, 64, 64), bf16),
        pltpu.VMEM((4, 4, 64, LANES), f32),
        pltpu.VMEM((4, 64, LANES), f32),
        pltpu.VMEM((3, 64, LANES), f32),
        pltpu.VMEM((4, 4, 2, 8, 1024), f32),
        pltpu.VMEM((4, 4, 8, 1024), f32),
        pltpu.VMEM((3, 4, 8, 1024), f32),
        pltpu.VMEM((4, 8, 1024), f32),
        pltpu.VMEM((3, 8, 1024), f32),
        pltpu.VMEM((64, 1024), f32),
        pltpu.VMEM((2, 8, LANES), f32),
        pltpu.VMEM((3, 3, 2, 8, LANES), f32),
        pltpu.VMEM((4, 8, WIDE), f32),
        pltpu.VMEM((2, 4, 8, WIDE), f32),
        pltpu.VMEM((4, 8, WIDE), f32),
        pltpu.VMEM((4, 8, WIDE), f32),
        pltpu.VMEM((3, 8, WIDE), f32),
        pltpu.VMEM((4, 8, WIDE), f32),
        pltpu.VMEM((4, 8, WIDE), f32),
        pltpu.VMEM((2, 4, 8, WIDE), f32),
        pltpu.VMEM((64, LANES), f32),
        dma,
        dma((9,)), dma((9,)), dma((9, 3)), dma((9, 3)), dma((9, 3)), dma((9, 3)), dma((9, 3)), dma((9, 3)),
        dma((7,)), dma((7,)), dma((17,)), dma((17,)), dma((3,)), dma((3,)), dma((10,)), dma((10,)),
    ]
    shapes = tuple(jax.ShapeDtypeStruct(v.shape, f32) for v in (src, rcv, off))
    parts = pl.pallas_call(
        kernel,
        out_shape=shapes,
        in_specs=[pl.BlockSpec(memory_space=pl.ANY)] + [vmem] * 7,
        out_specs=(vmem, vmem, vmem),
        scratch_shapes=scratch,
        compiler_params=pltpu.CompilerParams(vmem_limit_bytes=58 << 20, collective_id=0, has_side_effects=True),
        name="update",
    )(
        traces,
        trace_slot.reshape(16, LANES),
        trace_source.reshape(16, LANES),
        trace_offset.reshape(16, LANES),
        request_list.reshape(128, 8).T,
        src,
        rcv,
        off,
    )
    return pl.pallas_call(
        hand_over,
        out_shape=shapes,
        in_specs=[vmem] * 3,
        out_specs=(vmem,) * 3,
        name="hand_over",
    )(*parts)


def solution(mesh):
    every = P(("src", "rcv"))
    return jax.shard_map(
        local,
        mesh=mesh,
        in_specs=(P(("src", "rcv"), None), every, every, every, P(("src", "rcv"), None, None), P("src", None), P(("src", "rcv"), None), P()),
        out_specs=(P("src", None), P(("src", "rcv"), None), P()),
        check_vma=False,
    )
```

```python
import math

import jax
import jax.numpy as jnp
from jax import lax
from jax.experimental import pallas as pl
from jax.experimental.pallas import tpu as pltpu
from jax.sharding import PartitionSpec as P

NS = 2048
LANES = 128
ROWS = 1152
WIDE = 1024 + LANES
MESH = pl.DeviceIdType.MESH
KINDS = ((0, 1, 2, 0, 1, 2, 0, 1), (1, 2, 0, 1, 2, 0, 1, 2))
SECOND = ("y", "z", "x")
THIRD = ("z", "x", "y")
TN = (((0,), (0,)), ((), ()))
STEP = 2.0 * math.pi / NS
NT = (((1,), (1,)), ((), ()))


def trig_base(cb, sb):
    row = lax.broadcasted_iota(jnp.int32, (128, LANES), 0)
    col = lax.broadcasted_iota(jnp.int32, (128, LANES), 1)
    far = ((row * 16 * col) % NS).astype(jnp.float32) * STEP
    far_c, far_s = jnp.cos(far), jnp.sin(far)
    wide = (row * 16).astype(jnp.float32) * STEP
    wide_c, wide_s = jnp.cos(wide), jnp.sin(wide)
    row = lax.broadcasted_iota(jnp.int32, (16, LANES), 0)
    col = lax.broadcasted_iota(jnp.int32, (16, LANES), 1)
    near = ((row * col) % NS).astype(jnp.float32) * STEP
    near_c, near_s = jnp.cos(near), jnp.sin(near)
    half = (row.astype(jnp.float32) + 0.5) * STEP
    half_c, half_s = jnp.cos(half), jnp.sin(half)
    for b in range(128):
        fc, fs = far_c[b : b + 1], far_s[b : b + 1]
        wc, ws = wide_c[b : b + 1], wide_s[b : b + 1]
        taper = (0.5 - 0.5 * (wc * half_c - ws * half_s)) * (1.0 / math.sqrt(NS))
        cb[16 * b : 16 * b + 16, :] = taper * (fc * near_c - fs * near_s)
        sb[16 * b : 16 * b + 16, :] = taper * (fs * near_c + fc * near_s)


def chunk_table(c, rows, cb, sb, table):
    n = lax.broadcasted_iota(jnp.int32, (16, LANES), 0)
    turn = ((n * c) % 16).astype(jnp.float32) * (2.0 * math.pi / 16.0)
    tc, ts = jnp.cos(turn), jnp.sin(turn)
    for r in rows:
        bc, bs = cb[r : r + 16, :], sb[r : r + 16, :]
        table[r : r + 16, 0:LANES] = (bc * tc - bs * ts).astype(jnp.bfloat16)
        table[r : r + 16, LANES : 2 * LANES] = (-(bs * tc + bc * ts)).astype(jnp.bfloat16)


def split(x):
    upper = x.astype(jnp.bfloat16)
    return upper, (x - upper.astype(jnp.float32)).astype(jnp.bfloat16)


def kernel(
    tr_hbm, slot_ref, src_ref, off_ref, list_ref, s_ref, r_ref, o_ref,
    snew, rnew, onew,
    tr, hot, table, cb, sb, low, extra,
    grid, b1, b1d, b2, b2d, b3, pick,
    c2, comb, c3, us, e0, e1, v2, e2, uoff, own_list, far_list,
    ex, off, eo, ho, eh, eh2, eh3, fa, inv,
    tr_sem, s0s, s0r, s1s, s1r, s2s, s2r, s3s, s3r, us_s, us_r, os_s, os_r, xs_s, xs_r, ls_s, ls_r,
):
    f32, bf16 = jnp.float32, jnp.bfloat16
    group, x = lax.axis_index("src"), lax.axis_index("rcv")
    c, z, y = lax.rem(group, 2), lax.rem(group // 2, 4), group // 8
    me = {"x": x, "y": y, "z": z}

    def at(ax, k, flip=False):
        p = dict(me)
        if ax:
            p[ax] = lax.rem(p[ax] + k, 4)
        core = 1 - c if flip else c
        return ((p["y"] * 4 + p["z"]) * 2 + core, p["x"])

    def step(ax, k):
        return lax.rem(me[ax] + k, 4)

    twin = at(None, 0, True)
    peers = [twin] + [at(ax, k) for ax in "xyz" for k in (1, 2, 3)] + [at("x", k, True) for k in (1, 2, 3)]
    barrier = pltpu.get_barrier_semaphore()
    for p in peers:
        pl.semaphore_signal(barrier, inc=1, device_id=p, device_id_type=MESH)

    load = pltpu.make_async_copy(tr_hbm, tr, tr_sem)
    load.start()

    def rc(a, b, ss, rs, dev):
        return pltpu.make_async_remote_copy(
            src_ref=a, dst_ref=b, send_sem=ss, recv_sem=rs, device_id=dev, device_id_type=MESH
        )

    def start(copies):
        for cp in copies:
            cp.start()

    def wait(copies):
        for cp in copies:
            cp.wait()

    def x0(i):
        return [rc(grid.at[i, 2], grid.at[i, 1], s0s.at[i], s0r.at[i], twin)]

    def x1(i, kind, n):
        out = []
        for k in (1, 2, 3):
            j = step("xyz"[kind], k)
            part = (grid.at[i, 0:2, :, :, j], grid.at[i, 0:2, j], grid.at[i, 0:2, :, j])[kind]
            out.append(rc(part, b1.at[n, k - 1], s1s.at[n, k - 1], s1r.at[n, k - 1], at("xyz"[kind], k)))
        return out

    def x2(i, kind):
        ax = SECOND[kind]
        return [
            rc(b1d.at[i, step(ax, k)], b2.at[i, k - 1], s2s.at[i, k - 1], s2r.at[i, k - 1], at(ax, k))
            for k in (1, 2, 3)
        ]

    def x3(i, kind):
        ax = THIRD[kind]
        return [
            rc(b2d.at[i, step(ax, k)], b3.at[i, k - 1], s3s.at[i, k - 1], s3r.at[i, k - 1], at(ax, k))
            for k in (1, 2, 3)
        ]

    def c_x2(a):
        return [rc(b1d.at[8, step(a, k)], c2.at[k], s2s.at[8, k - 1], s2r.at[8, k - 1], at(a, k)) for k in (1, 2, 3)]

    def c_x3(b):
        return [rc(comb.at[step(b, k)], c3.at[k - 1], s3s.at[8, k - 1], s3r.at[8, k - 1], at(b, k)) for k in (1, 2, 3)]

    def list_0():
        return [rc(own_list.at[0], own_list.at[1], ls_s.at[9], ls_r.at[9], twin)]

    def list_1():
        return [
            rc(own_list, far_list.at[n, k - 1], ls_s.at[3 * n + k - 1], ls_r.at[3 * n + k - 1], at(ax, k))
            for n, ax in enumerate("xyz")
            for k in (1, 2, 3)
        ]

    def u_core():
        return [rc(us.at[:, :, 1], e0, us_s.at[0], us_r.at[0], twin)]

    def u_near(a):
        return [rc(us.at[:, k, 0], e1.at[k - 1], us_s.at[k], us_r.at[k], at(a, 4 - k)) for k in (1, 2, 3)]

    def u_far(b):
        return [rc(v2.at[k], e2.at[k - 1], us_s.at[3 + k], us_r.at[3 + k], at(b, 4 - k)) for k in (1, 2, 3)]

    def src_x():
        return [rc(ex.at[x], ex.at[x], xs_s.at[k - 1], xs_r.at[k - 1], at("x", k)) for k in (1, 2, 3)]

    def off_core():
        return [rc(off.at[1 - c], eo, os_s.at[0], os_r.at[0], twin)]

    def off_x():
        return [rc(ho.at[step("x", k)], eh.at[k - 1], os_s.at[k], os_r.at[k], at("x", k)) for k in (1, 2, 3)]

    def off_y():
        return [rc(eh2.at[y], eh2.at[y], os_s.at[3 + k], os_r.at[3 + k], at("y", k)) for k in (1, 2, 3)]

    def off_z():
        return [rc(eh3.at[z], eh3.at[z], os_s.at[6 + k], os_r.at[6 + k], at("z", k)) for k in (1, 2, 3)]

    def off_all():
        to = [at("x", k) for k in (1, 2, 3)] + [twin] + [at("x", k, True) for k in (1, 2, 3)]
        return [rc(fa.at[c, x], fa.at[c, x], os_s.at[10 + n], os_r.at[10 + n], d) for n, d in enumerate(to)]

    s = slot_ref[...]
    row_of = (
        (((s >> 5) & 1) ^ c) * 512 + (s >> 8) * 128 + ((s >> 6) & 3) * 32 + ((s >> 3) & 3) * 8 + (s & 7)
    )
    first = src_ref[...] - group * 8 + 1024
    second = off_ref[...] + 1032

    def hot_rows(i, _):
        r = pl.multiple_of(i * 32, 32)
        row = lax.broadcasted_iota(jnp.int32, (32, LANES), 0) + r
        for b in range(16):
            hit = row == row_of[b : b + 1, :]
            hot[pl.ds(r, 32), b * LANES : (b + 1) * LANES] = jnp.where(hit, 1.0, 0.0).astype(bf16)
        return 0

    lax.fori_loop(0, 32, hot_rows, 0)
    for r in range(1024, ROWS, 32):
        row = lax.broadcasted_iota(jnp.int32, (32, LANES), 0) + r
        for b in range(16):
            hit = (row == first[b : b + 1, :]) | (row == second[b : b + 1, :])
            hot[r : r + 32, b * LANES : (b + 1) * LANES] = jnp.where(hit, 1.0, 0.0).astype(bf16)

    cnt = lax.dot_general(hot[:, 0:NS], hot[1024:ROWS, 0:NS], NT, preferred_element_type=f32)
    upper, lower = split(cnt)
    hot[:, NS : NS + LANES] = upper
    hot[:, NS + LANES : NS + 2 * LANES] = lower
    low[NS + 72 : NS + 128, :] = jnp.zeros((56, 2 * LANES), bf16)
    low[NS + 200 : NS + 256, :] = jnp.zeros((56, 2 * LANES), bf16)
    lane = lax.broadcasted_iota(jnp.int32, (1, LANES), 1)
    count_s = jnp.sum(jnp.where((lane >= 8) & (lane < 72), cnt[1024:1032], 0.0), axis=1, keepdims=True)
    count_o = jnp.sum(jnp.where(lane < 8, cnt[1032:1096], 0.0), axis=1, keepdims=True)
    extra[0:8, 1024:WIDE] = jnp.broadcast_to(count_s, (8, LANES))
    extra[8:72, 1024:WIDE] = jnp.broadcast_to(count_o, (64, LANES))

    grid[8, 0] = cnt[0:512].reshape(4, 4, 4, 8, LANES)
    far = cnt[512:1024]
    far = jnp.where((lane >= 80) & (lane < 88), pltpu.roll(far, 80, 1), jnp.where(lane < 8, 0.0, far))
    grid[8, 2] = far.reshape(4, 4, 4, 8, LANES)
    own_list[0] = list_ref[...].astype(f32)

    pl.semaphore_wait(barrier, len(peers))
    start(list_0())
    start(x0(8))
    trig_base(cb, sb)
    load.wait()

    def rows64(i, n, kind, p, q):
        own = (
            grid[i, 0:2, p, q, x] if kind == 0 else grid[i, 0:2, y, p, q] if kind == 1 else grid[i, 0:2, p, z, q]
        )
        return jnp.concatenate([own.reshape(16, LANES), b1[n, :, :, p, q].reshape(48, LANES)], axis=0)

    def densify(i, n, kind, swap=False):
        def one(m, _):
            p, q = m // 4, lax.rem(m, 4)
            upper, lower = split(rows64(i, n, kind, p, q))
            both = jnp.concatenate([upper, lower], axis=1)
            out = jnp.dot(pick[kind, m], both, preferred_element_type=f32)
            total = out[:, 0:LANES] + out[:, LANES:]
            if kind == 2 or swap:
                b1d[i, q, p] = total
            else:
                b1d[i, p, q] = total
            return 0

        lax.fori_loop(0, 16, one, 0, unroll=4)

    def counts_1():
        wait(list_0())
        start(list_1())
        wait(x0(8))
        start(x1(8, 0, 8))

    def lists():
        wait(list_1())
        row = lax.broadcasted_iota(jnp.int32, (1024, LANES), 0)
        col = lax.broadcasted_iota(jnp.int32, (1024, LANES), 1)
        p, q = row >> 8, (row >> 6) & 3
        want = (lax.broadcasted_iota(jnp.int32, (1024, 64), 0) & 63).astype(f32)
        for kind in range(3):
            py, pz, px = ((p, q, x), (y, p, q), (p, z, q))[kind]
            owner = ((py * 4 + pz) * 2 + c) * 4 + px
            which = jnp.where(col == owner, 1.0, 0.0).astype(bf16)
            rows = jnp.concatenate([own_list[...].reshape(16, LANES), far_list[kind].reshape(48, LANES)], axis=0)
            named = lax.dot_general(which, rows.astype(bf16), NT, preferred_element_type=f32)
            pick[kind] = jnp.where(named == want, 1.0, 0.0).astype(bf16).reshape(16, 64, 64)

    def by_core(f):
        for core, axes in enumerate((("y", "z"), ("z", "y"))):
            @pl.when(c == core)
            def _(axes=axes):
                f(*axes)

    def counts_2():
        wait(x1(8, 0, 8))

        def go(a, b):
            densify(8, 8, 0, swap=a == "z")
            start(c_x2(a))

        by_core(go)

    def counts_3():
        def go(a, b):
            wait(c_x2(a))
            c2[0] = b1d[8, me[a]]
            total = jnp.zeros((256, LANES), f32)
            for k in range(4):
                mm = c2[k].reshape(256, LANES)
                total = total + pltpu.roll(jnp.where((lane >= 8) & (lane < 72), mm, 0.0), 120, 1)
                total = total + pltpu.roll(jnp.where(lane < 8, mm, 0.0), 64 + 16 * k, 1)
                moved = (16 * k + 120) % 128
                one = jnp.where((lane >= 80) & (lane < 88), mm, 0.0)
                total = total + (pltpu.roll(one, moved, 1) if moved else one)
            comb[...] = total.reshape(4, 64, LANES)
            start(c_x3(b))

        by_core(go)

    def counts_4():
        by_core(lambda a, b: wait(c_x3(b)))
        parts = [comb[jnp.where(c == 0, z, y)], c3[0], c3[1], c3[2]]
        offs = jnp.where(lane < 64, parts[0] + parts[1] + parts[2] + parts[3], 0.0)
        hits = jnp.sum(offs, axis=1, keepdims=True)
        inv[...] = jnp.broadcast_to(1.0 / (hits + 1.0), (64, LANES))
        high = [jnp.where(lane >= 64, v, 0.0) for v in parts]
        wide = jnp.concatenate([pltpu.roll(high[0], 64, 1) + high[1], pltpu.roll(high[2], 64, 1) + high[3], offs], axis=1)
        upper, lower = split(wide)
        left = jnp.concatenate([upper, lower], axis=0)
        for h in range(4):
            r1, r2 = split(r_ref[:, h * 256 : h * 256 + 256])
            both = jnp.concatenate([r1, r2], axis=1)
            out = lax.dot_general(left, jnp.concatenate([both, both], axis=0), TN, preferred_element_type=f32)
            u = out[:, 0:256] + out[:, 256:]
            us[:, :, :, :, h * 256 : h * 256 + 256] = u[0:256].reshape(4, 4, 2, 8, 256)
            uoff[:, h * 256 : h * 256 + 256] = u[256:320]
        start(u_core())

    def counts_5():
        wait(u_core())
        for p in range(4):
            for q in range(4):
                us[p, q, 0] = us[p, q, 0] + e0[q, p]
        by_core(lambda a, b: start(u_near(a)))

    def counts_6():
        by_core(lambda a, b: wait(u_near(a)))
        v2[...] = us[:, 0, 0] + e1[0] + e1[1] + e1[2]
        by_core(lambda a, b: start(u_far(b)))

    def counts_7():
        by_core(lambda a, b: wait(u_far(b)))
        ex[x, :, 0:1024] = extra[0:8, 0:1024] - (v2[0] + e2[0] + e2[1] + e2[2])
        ex[x, :, 1024:WIDE] = extra[0:8, 1024:WIDE]
        start(src_x())

    def each_core(i, f):
        for core in (0, 1):
            @pl.when(c == core)
            def _(kind=KINDS[core][i]):
                f(kind)

    def w0(i):
        wait(x0(i))
        each_core(i, lambda kind: start(x1(i, kind, i)))

    def w1(i):
        def go(kind):
            wait(x1(i, kind, i))
            densify(i, i, kind)
            start(x2(i, kind))

        each_core(i, go)

    def w2(i):
        def go(kind):
            wait(x2(i, kind))
            b2d[i] = b1d[i, me[SECOND[kind]]] + b2[i, 0] + b2[i, 1] + b2[i, 2]
            start(x3(i, kind))

        each_core(i, go)

    def w3(i):
        def go(kind):
            wait(x3(i, kind))
            total = b2d[i, me[THIRD[kind]]] + b3[i, 0] + b3[i, 1] + b3[i, 2]
            cols = slice(i * LANES, (i + 1) * LANES)
            rnew[:, cols] = (r_ref[:, cols] + total) * inv[...]

        each_core(i, go)

    def later(f, n):
        return lambda: f(n)

    first = {
        2: [lists],
    }
    mid = {
        0: [counts_1],
        3: [later(w1, 0)],
        4: [later(w1, 1)],
        5: [later(w1, 2), later(w2, 0)],
        6: [later(w1, 3), later(w2, 1)],
        7: [later(w1, 4), later(w2, 2)],
    }
    end = {
        1: [later(w0, 0)],
        2: [later(w0, 1), counts_2],
        3: [later(w0, 2)],
        4: [later(w0, 3), counts_3],
        5: [later(w0, 4), counts_4],
        6: [later(w0, 5), later(w3, 0), counts_5],
        7: [later(w0, 6), later(w3, 1)],
    }

    def point(i, table_of):
        for n, todo in table_of.items():
            @pl.when(i == n)
            def _(todo=todo):
                for f in todo:
                    f()

    def chunk(i, _):
        at_lane = pl.multiple_of(i * LANES, LANES)
        point(i, first)
        chunk_table(i, range(0, NS, 16), cb, sb, table)
        for r in range(0, NS, 256):
            spec = jnp.dot(tr[r : r + 256, :], table[...], preferred_element_type=f32)
            re, im = spec[:, 0:LANES], spec[:, LANES:]
            amp = 0.5 * jnp.log(re * re + im * im + 0.01)
            upper, lower = split(amp)
            low[r : r + 256, 0:LANES] = upper
            low[r : r + 256, LANES:] = lower
        terms = jnp.concatenate([s_ref[:, pl.ds(at_lane, LANES)], o_ref[:, pl.ds(at_lane, LANES)]], axis=0)
        upper, lower = split(-terms)
        for r in (NS, NS + LANES):
            low[r : r + 72, 0:LANES] = upper
            low[r : r + 72, LANES:] = lower
        point(i, mid)
        for half in (0, 1):
            out = jnp.dot(hot[half * 512 : half * 512 + 512, :], low[...], preferred_element_type=f32)
            grid[i, 2 * half] = (out[:, 0:LANES] + out[:, LANES:]).reshape(4, 4, 4, 8, LANES)
        out = jnp.dot(hot[1024:ROWS, :], low[...], preferred_element_type=f32)
        extra[:, pl.ds(at_lane, LANES)] = (out[:, 0:LANES] + out[:, LANES:])[0:72]
        for n in range(8):
            @pl.when(i == n)
            def _(n=n):
                start(x0(n))
                for f in end.get(n, []):
                    f()
        return 0

    lax.fori_loop(0, 8, chunk, 0)

    off[:, :, :, 0:1024] = (extra[8:72, 0:1024] - uoff[...]).reshape(2, 4, 8, 1024)
    off[:, :, :, 1024:WIDE] = extra[8:72, 1024:WIDE].reshape(2, 4, 8, LANES)
    start(off_core())
    counts_6()
    w1(5)
    w2(3)
    w0(7)
    w3(2)
    wait(off_core())
    ho[...] = off[c] + eo[...]
    start(off_x())
    w1(6)
    w2(4)
    counts_7()
    wait(off_x())
    eh2[y] = ho[x] + eh[0] + eh[1] + eh[2]
    start(off_y())
    w3(3)
    w1(7)
    w2(5)
    wait(off_y())
    eh3[z] = eh2[0] + eh2[1] + eh2[2] + eh2[3]
    start(off_z())
    w3(4)
    w2(6)
    wait(off_z())
    fa[c, x] = eh3[0] + eh3[1] + eh3[2] + eh3[3]
    start(off_all())
    w3(5)
    w2(7)
    wait(off_all())
    total = fa[...].reshape(64, WIDE)
    onew[...] = o_ref[...] + total[:, 0:1024] / (total[:, 1024:1025] + 1.0)
    w3(6)
    wait(src_x())
    total = ex[0] + ex[1] + ex[2] + ex[3]
    snew[...] = s_ref[...] + total[:, 0:1024] / (total[:, 1024:1025] + 1.0)
    w3(7)


def hand_over(a, b, d, oa, ob, od):
    oa[...] = a[...]
    ob[...] = b[...]
    od[...] = d[...]


def local(traces, trace_source, trace_offset, trace_slot, request_list, src, rcv, off):
    f32, bf16 = jnp.float32, jnp.bfloat16
    vmem = pl.BlockSpec(memory_space=pltpu.VMEM)
    dma = pltpu.SemaphoreType.DMA
    scratch = [
        pltpu.VMEM((NS, NS), bf16),
        pltpu.VMEM((ROWS, NS + 256), bf16),
        pltpu.VMEM((NS, 256), bf16),
        pltpu.VMEM((NS, LANES), f32),
        pltpu.VMEM((NS, LANES), f32),
        pltpu.VMEM((NS + 256, 256), bf16),
        pltpu.VMEM((72, WIDE), f32),
        pltpu.VMEM((9, 3, 4, 4, 4, 8, LANES), f32),
        pltpu.VMEM((9, 3, 2, 4, 4, 8, LANES), f32),
        pltpu.VMEM((9, 4, 4, 64, LANES), f32),
        pltpu.VMEM((8, 3, 4, 64, LANES), f32),
        pltpu.VMEM((8, 4, 64, LANES), f32),
        pltpu.VMEM((8, 3, 64, LANES), f32),
        pltpu.VMEM((3, 16, 64, 64), bf16),
        pltpu.VMEM((4, 4, 64, LANES), f32),
        pltpu.VMEM((4, 64, LANES), f32),
        pltpu.VMEM((3, 64, LANES), f32),
        pltpu.VMEM((4, 4, 2, 8, 1024), f32),
        pltpu.VMEM((4, 4, 8, 1024), f32),
        pltpu.VMEM((3, 4, 8, 1024), f32),
        pltpu.VMEM((4, 8, 1024), f32),
        pltpu.VMEM((3, 8, 1024), f32),
        pltpu.VMEM((64, 1024), f32),
        pltpu.VMEM((2, 8, LANES), f32),
        pltpu.VMEM((3, 3, 2, 8, LANES), f32),
        pltpu.VMEM((4, 8, WIDE), f32),
        pltpu.VMEM((2, 4, 8, WIDE), f32),
        pltpu.VMEM((4, 8, WIDE), f32),
        pltpu.VMEM((4, 8, WIDE), f32),
        pltpu.VMEM((3, 8, WIDE), f32),
        pltpu.VMEM((4, 8, WIDE), f32),
        pltpu.VMEM((4, 8, WIDE), f32),
        pltpu.VMEM((2, 4, 8, WIDE), f32),
        pltpu.VMEM((64, LANES), f32),
        dma,
        dma((9,)), dma((9,)), dma((9, 3)), dma((9, 3)), dma((9, 3)), dma((9, 3)), dma((9, 3)), dma((9, 3)),
        dma((7,)), dma((7,)), dma((17,)), dma((17,)), dma((3,)), dma((3,)), dma((10,)), dma((10,)),
    ]
    shapes = tuple(jax.ShapeDtypeStruct(v.shape, f32) for v in (src, rcv, off))
    parts = pl.pallas_call(
        kernel,
        out_shape=shapes,
        in_specs=[pl.BlockSpec(memory_space=pl.ANY)] + [vmem] * 7,
        out_specs=(vmem, vmem, vmem),
        scratch_shapes=scratch,
        compiler_params=pltpu.CompilerParams(vmem_limit_bytes=58 << 20, collective_id=0, has_side_effects=True),
        name="update",
    )(
        traces,
        trace_slot.reshape(16, LANES),
        trace_source.reshape(16, LANES),
        trace_offset.reshape(16, LANES),
        request_list.reshape(128, 8).T,
        src,
        rcv,
        off,
    )
    return pl.pallas_call(
        hand_over,
        out_shape=shapes,
        in_specs=[vmem] * 3,
        out_specs=(vmem,) * 3,
        name="hand_over",
    )(*parts)


def solution(mesh):
    every = P(("src", "rcv"))
    return jax.shard_map(
        local,
        mesh=mesh,
        in_specs=(P(("src", "rcv"), None), every, every, every, P(("src", "rcv"), None, None), P("src", None), P(("src", "rcv"), None), P()),
        out_specs=(P("src", None), P(("src", "rcv"), None), P()),
        check_vma=False,
    )
```
